256 devices in a mesh: sp: 64 (over y, z, x_hi), ch: 4 (over x_lo, core).
Axes of the slice: x: 4 (x_hi: 2, x_lo: 2; x = x_hi * 2 + x_lo), y: 4, z: 8, core: 2. Of those that a mesh axis runs over, the one named last changes fastest.
Arguments:
- field: bfloat16 [32, 64, 32, 4096], P('ch', 'sp'), may hold values from -6 to 6
- spectral_weight: bfloat16 [16, 2048, 1024], P(None, ('sp', 'ch')), may hold values from -1 to 1
- point_weight: bfloat16 [32, 32], replicated, may hold values from -1 to 1
- bias: float32 [32], replicated, may hold values from -3 to 3
- cotangent: bfloat16 [32, 64, 32, 4096], P('ch', 'sp'), may hold values from -6 to 6
Outputs:
- activated: bfloat16 [32, 64, 32, 4096], P('ch', 'sp')
- field_grad: bfloat16 [32, 64, 32, 4096], P('ch', 'sp')
- spectral_grad: float32 [16, 2048, 1024], P(None, ('sp', 'ch'))
- weight_grad: float32 [32, 32], replicated
- bias_grad: float32 [32], replicated
The draws below stay inside these ranges and needn't reach their ends.
All inputs are finite; a program needn't handle non-finite values.
Results may differ from the reference program's by a relative error of at most 0.0065.
Values sent between devices are 32-bit elements; how exact they have to be, the bound alone decides.
A program may use at most 64 MiB of HBM per device.

```python
import math
import jax
import jax.numpy as jnp
from jax import lax

WIDTH = 32
KX = 16
KY = 16
KZ = 16
KT = 8
GY = 64
GZ = 64
GT = 32
GX = 64
KYZ = 256
Q = 2048


def shard_levels(own_key, dims, cuts, low, top_value):
    loudness = 1.0
    for axis_at, parts in cuts:
        steps = jax.random.uniform(jax.random.fold_in(jax.random.fold_in(own_key, 6), axis_at), (parts,), jnp.float32, low / len(cuts), top_value / len(cuts))
        loudness = loudness * jnp.repeat(jnp.exp(steps), dims[axis_at] // parts).reshape((-1,) + (1,) * (len(dims) - 1 - axis_at))
    return loudness


def normal_values(rng, dims, scale, most, pieces=(), kind=jnp.bfloat16):
    gain = shard_levels(rng, dims, pieces, -0.22, 0.18) if pieces else 1.0
    result = jax.random.normal(rng, dims, jnp.float32) * scale * gain
    return jnp.minimum(jnp.maximum(result, -most), most).astype(kind)


def setup_inputs(seed: int = 0) -> dict:
    key_of = jax.random.split(jax.random.key(seed), 6)
    return {
        "field": normal_values(key_of[0], (GT, GX, WIDTH, GY * GZ), 1.0, 6.0, ((0, 4), (1, 64))),
        "spectral_weight": normal_values(key_of[1], (KX, Q, WIDTH * WIDTH), WIDTH ** -0.5, 1.0, ((1, 256),)),
        "point_weight": normal_values(key_of[2], (WIDTH, WIDTH), WIDTH ** -0.5, 1.0),
        "bias": normal_values(key_of[3], (WIDTH,), 0.5, 3.0, (), jnp.float32),
        "cotangent": normal_values(key_of[4], (GT, GX, WIDTH, GY * GZ), 1.0, 6.0, ((0, 4), (1, 64))),
    }


PRECISE = lax.Precision.HIGHEST
SQRT_HALF = 0.7071067811865476
INV_ROOT_TWO_PI = 0.3989422804014327

def wave_table(length, kept_rows, positions):
    row_ids = jnp.arange(kept_rows, dtype=jnp.int32)
    half_kept = kept_rows // 2
    frequency = jnp.where(row_ids <= half_kept, row_ids, row_ids - half_kept)
    phase_ids = frequency[:, None] * positions[None, :] % length
    angles = 2.0 * math.pi / length * phase_ids.astype(jnp.float32)
    waves = jnp.where((row_ids <= half_kept)[:, None], jnp.cos(angles), jnp.sin(angles))
    return math.sqrt(2.0 / length) * waves

def plane_tables():
    wave_y = wave_table(GY, KY, jnp.arange(GY, dtype=jnp.int32))
    wave_z = wave_table(GZ, KZ, jnp.arange(GZ, dtype=jnp.int32))
    forward = (wave_y[:, None, :, None] * wave_z[None, :, None, :]).reshape(KY * KZ, GY * GZ)
    scaled_y = wave_y * math.sqrt(GY / KY)
    scaled_z = wave_z * math.sqrt(GZ / KZ)
    inverse = (scaled_y[:, None, :, None] * scaled_z[None, :, None, :]).reshape(KY * KZ, GY * GZ)
    return (forward.astype(jnp.bfloat16), inverse.astype(jnp.bfloat16))

def gelu_slope(values):
    return 0.5 * (1.0 + lax.erf(values * SQRT_HALF)) + values * jnp.exp(-0.5 * values * values) * INV_ROOT_TWO_PI

def reference(field, spectral_weight, point_weight, bias, cotangent):
    forward_x = wave_table(GX, KX, jnp.arange(GX, dtype=jnp.int32))
    inverse_x = forward_x * math.sqrt(GX / KX)
    forward_t = wave_table(GT, KT, jnp.arange(GT, dtype=jnp.int32))
    inverse_t = forward_t * math.sqrt(GT / KT)
    forward_yz, inverse_yz = plane_tables()
    plane_cells = GY * GZ

    def plane_forward(time_slab):
        return jnp.dot(time_slab.reshape(-1, plane_cells), forward_yz.T, preferred_element_type=jnp.float32).reshape(GX, WIDTH, KYZ)
    plane_coeffs = lax.map(plane_forward, field)
    coeffs = jnp.einsum('kt,lx,txcq->lckq', forward_t, forward_x, plane_coeffs, precision=PRECISE).reshape(KX, WIDTH, Q)
    weights = spectral_weight.reshape(KX, Q, WIDTH, WIDTH)

    def mix_one(operands):
        return jnp.einsum('iq,qio->oq', operands[0], operands[1].astype(jnp.float32), precision=PRECISE)
    mixed_modes = lax.map(mix_one, (coeffs, weights))
    spread_modes = jnp.einsum('kt,lx,lokq->txoq', inverse_t, inverse_x, mixed_modes.reshape(KX, WIDTH, KT, KYZ), precision=PRECISE)
    inverse_table = inverse_yz.astype(jnp.float32)
    point_f32 = point_weight.astype(jnp.float32)

    def forward_step(totals, slices):
        time_slab, cotan_slab, mode_slab = slices
        spatial = jnp.dot(mode_slab.reshape(-1, KYZ), inverse_table, precision=PRECISE).reshape(GX, WIDTH, plane_cells)
        slab_f32 = time_slab.astype(jnp.float32)
        linear = jnp.einsum('xiy,io->xoy', slab_f32, point_f32, precision=PRECISE)
        preact = spatial + linear + bias[None, :, None]
        activation = jax.nn.gelu(preact, approximate=False).astype(jnp.bfloat16)
        slopes = (cotan_slab.astype(jnp.float32) * gelu_slope(preact)).astype(jnp.bfloat16)
        slopes_f32 = slopes.astype(jnp.float32)
        weight_sum = totals[0] + jnp.einsum('xiy,xoy->io', slab_f32, slopes_f32, precision=PRECISE)
        bias_sum = totals[1] + lax.optimization_barrier(jnp.sum(slopes_f32, axis=(0, 2)))
        projected = jnp.dot(slopes.reshape(-1, plane_cells), inverse_yz.T, preferred_element_type=jnp.float32).reshape(GX, WIDTH, KYZ)
        return ((weight_sum, bias_sum), (activation, slopes, projected))
    start_totals = (jnp.zeros((WIDTH, WIDTH), jnp.float32), jnp.zeros((WIDTH,), jnp.float32))
    sums, outputs = lax.scan(forward_step, start_totals, (field, cotangent, spread_modes))
    activated, slopes_all, projected_all = outputs
    slope_modes = jnp.einsum('kt,lx,txoq->lokq', inverse_t, inverse_x, projected_all, precision=PRECISE).reshape(KX, WIDTH, Q)
    cell_scale = 1.0 / math.sqrt(GX * GY * GZ * GT)
    spec_scale = math.sqrt(KX * Q / (GX * GY * GZ * GT))
    spectral_grad = (spec_scale * jnp.einsum('kiq,koq->kqio', coeffs, slope_modes)).reshape(KX, Q, WIDTH * WIDTH)
    weight_grad = cell_scale * sums[0]
    bias_grad = cell_scale * sums[1]

    def adjoint_one(operands):
        return jnp.einsum('qio,oq->iq', operands[0].astype(jnp.float32), operands[1], precision=PRECISE)
    coeff_grad = lax.map(adjoint_one, (weights, slope_modes))
    grad_modes = jnp.einsum('kt,lx,likq->txiq', forward_t, forward_x, coeff_grad.reshape(KX, WIDTH, KT, KYZ), precision=PRECISE)
    forward_table = forward_yz.astype(jnp.float32)

    def back_step(unused, slices):
        slope_slab, mode_slab = slices
        spectral_part = jnp.dot(mode_slab.reshape(-1, KYZ), forward_table, precision=PRECISE).reshape(GX, WIDTH, plane_cells)
        point_part = jnp.einsum('xoy,io->xiy', slope_slab.astype(jnp.float32), point_f32, precision=PRECISE)
        return (unused, (spectral_part + point_part).astype(jnp.bfloat16))
    unused_end, field_grad = lax.scan(back_step, jnp.zeros((), jnp.float32), (slopes_all, grad_modes))
    return (activated, field_grad, spectral_grad, weight_grad, bias_grad)
```

```python
import math

import jax
import jax.numpy as jnp
from jax import lax
from jax.sharding import PartitionSpec as P

KX = 16
KY = 16
KZ = 16
KT = 8
GY = 64
GZ = 64
GT = 32
KYZ = 256
Q = 2048


PRECISE = lax.Precision.HIGHEST
SQRT_HALF = 0.7071067811865476
INV_ROOT_TWO_PI = 0.3989422804014327


def wave_table(length, kept_rows, positions):
    row_ids = jnp.arange(kept_rows, dtype=jnp.int32)
    half_kept = kept_rows // 2
    frequency = jnp.where(row_ids <= half_kept, row_ids, row_ids - half_kept)
    phase_ids = frequency[:, None] * positions[None, :] % length
    angles = 2.0 * math.pi / length * phase_ids.astype(jnp.float32)
    waves = jnp.where((row_ids <= half_kept)[:, None], jnp.cos(angles), jnp.sin(angles))
    return math.sqrt(2.0 / length) * waves


def plane_tables():
    wave_y = wave_table(GY, KY, jnp.arange(GY, dtype=jnp.int32))
    wave_z = wave_table(GZ, KZ, jnp.arange(GZ, dtype=jnp.int32))
    scaled_y = wave_y * math.sqrt(GY / KY)
    scaled_z = wave_z * math.sqrt(GZ / KZ)
    wave_y, wave_z, scaled_y, scaled_z = lax.optimization_barrier((wave_y, wave_z, scaled_y, scaled_z))
    forward = (wave_y[:, None, :, None] * wave_z[None, :, None, :]).reshape(KY * KZ, GY * GZ)
    inverse = (scaled_y[:, None, :, None] * scaled_z[None, :, None, :]).reshape(KY * KZ, GY * GZ)
    return (forward.astype(jnp.bfloat16), inverse.astype(jnp.bfloat16))


def split_dot(values, table):
    high = values.astype(jnp.bfloat16)
    low = (values - high.astype(jnp.float32)).astype(jnp.bfloat16)
    return jnp.dot(high, table, preferred_element_type=jnp.float32) + jnp.dot(
        low, table, preferred_element_type=jnp.float32
    )


def gelu_slope(values):
    return (
        0.5 * (1.0 + lax.erf(values * SQRT_HALF))
        + values * jnp.exp(-0.5 * values * values) * INV_ROOT_TWO_PI
    )


def to_spectrum(values, yz_table, time_table, x_table, sp_count, extra=None):
    steps_here, planes, channels, plane_cells = values.shape
    grid_x = planes * sp_count
    flat_rows = jnp.einsum(
        "rc,qc->rq", values.reshape(-1, plane_cells), yz_table, preferred_element_type=jnp.float32
    )
    partial_value = jnp.einsum(
        "kt,txcq->xckq",
        time_table,
        flat_rows.reshape(steps_here, planes, channels, KYZ),
        precision=PRECISE,
    )
    partial_value = partial_value.reshape(planes, channels, Q)
    if extra is not None:
        partial_value = jnp.concatenate([partial_value, extra.reshape(1, 1, Q)], axis=1)
    arrived = lax.all_to_all(partial_value, "sp", split_axis=2, concat_axis=0, tiled=True)
    if extra is not None:
        extra_sum = jnp.sum(arrived[:, channels, :], axis=0)
        arrived = arrived[:, :channels, :]
    x_modes = jnp.dot(x_table, arrived.reshape(grid_x, -1), precision=PRECISE).reshape(
        KX, channels, -1
    )
    if extra is None:
        return lax.psum_scatter(x_modes, "ch", scatter_dimension=2, tiled=True)
    extra_row = jnp.zeros((1, channels, extra_sum.shape[0]), jnp.float32).at[0, 0, :].set(extra_sum)
    scattered = lax.psum_scatter(
        jnp.concatenate([x_modes, extra_row], axis=0), "ch", scatter_dimension=2, tiled=True
    )
    return scattered[:KX], scattered[KX, 0, :]


def to_planes(coeff_block, x_table, time_table, yz_table, planes, sp_count, extra=None):
    channels = coeff_block.shape[1]
    grid_x = planes * sp_count
    if extra is not None:
        extra_row = jnp.zeros((1, channels, extra.shape[0]), jnp.float32).at[0, 0, :].set(extra)
        coeff_block = jnp.concatenate([coeff_block, extra_row], axis=0)
    all_modes = lax.all_gather(coeff_block, "ch", axis=2, tiled=True)
    spread = jnp.einsum(
        "kx,kr->xr", x_table, all_modes[:KX].reshape(KX, -1), precision=PRECISE
    ).reshape(grid_x, channels, -1)
    if extra is not None:
        gathered = jnp.broadcast_to(all_modes[KX, 0, :], (grid_x, 1, all_modes.shape[2]))
        spread = jnp.concatenate([spread, gathered], axis=1)
    returned = lax.all_to_all(spread, "sp", split_axis=0, concat_axis=2, tiled=True)
    extra_total = returned[0, channels, :] if extra is not None else None
    returned = returned[:, :channels].reshape(planes, channels, KT, KYZ)
    time_spread = jnp.einsum("kt,xckq->txcq", time_table, returned, precision=PRECISE)
    steps_here = time_table.shape[1]
    result = split_dot(time_spread.reshape(-1, KYZ), yz_table)
    return result.reshape(steps_here, planes, channels, -1), extra_total


def shards(field, spectral_weight, point_weight, bias, cotangent):
    steps_here, planes, channels, plane_cells = field.shape
    sp_count = lax.axis_size("sp")
    grid_x = planes * sp_count
    forward_x = wave_table(grid_x, KX, jnp.arange(grid_x, dtype=jnp.int32))
    inverse_x = forward_x * math.sqrt(grid_x / KX)
    time_ids = lax.axis_index("ch") * steps_here + jnp.arange(steps_here, dtype=jnp.int32)
    forward_t = wave_table(GT, KT, time_ids)
    inverse_t = forward_t * math.sqrt(GT / KT)
    forward_yz, inverse_yz = plane_tables()
    coeffs = to_spectrum(field, forward_yz, forward_t, forward_x, sp_count)
    weights = spectral_weight.reshape(KX, -1, channels, channels).astype(jnp.float32)
    mixed_modes = jnp.einsum("kiq,kqio->koq", coeffs, weights, precision=PRECISE)
    spatial, _ = to_planes(mixed_modes, inverse_x, inverse_t, inverse_yz, planes, sp_count)
    field_rows = field.reshape(-1, channels, plane_cells)
    linear = jnp.einsum(
        "io,riy->roy", point_weight, field_rows, preferred_element_type=jnp.float32
    ).reshape(spatial.shape)
    preact = spatial + linear + bias[None, None, :, None]
    activated = jax.nn.gelu(preact, approximate=False).astype(jnp.bfloat16)
    slopes = (cotangent.astype(jnp.float32) * gelu_slope(preact)).astype(jnp.bfloat16)
    slope_rows = slopes.reshape(-1, channels, plane_cells)
    weight_part = jnp.einsum("riy,roy->io", field_rows, slope_rows, preferred_element_type=jnp.float32)
    bias_part = jnp.sum(slopes.astype(jnp.float32), axis=(0, 1, 3))
    packed = jnp.concatenate([weight_part.reshape(-1), bias_part])
    packed = jnp.pad(packed, (0, Q - packed.shape[0]))
    slope_modes, packed_part = to_spectrum(
        slopes, inverse_yz, inverse_t, inverse_x, sp_count, extra=packed
    )
    spec_scale = math.sqrt(KX * Q / (grid_x * GY * GZ * GT))
    spectral_grad = (spec_scale * jnp.einsum("kiq,koq->kqio", coeffs, slope_modes)).reshape(
        KX, -1, channels * channels
    )
    coeff_grad = jnp.einsum("kqio,koq->kiq", weights, slope_modes, precision=PRECISE)
    grad_spatial, packed_sum = to_planes(
        coeff_grad, forward_x, forward_t, forward_yz, planes, sp_count, extra=packed_part
    )
    cell_scale = 1.0 / math.sqrt(grid_x * GY * GZ * GT)
    weight_grad = cell_scale * packed_sum[: channels * channels].reshape(channels, channels)
    bias_grad = cell_scale * packed_sum[channels * channels : channels * channels + channels]
    point_part = jnp.einsum(
        "io,roy->riy", point_weight, slope_rows, preferred_element_type=jnp.float32
    ).reshape(grad_spatial.shape)
    field_grad = (grad_spatial + point_part).astype(jnp.bfloat16)
    return (activated, field_grad, spectral_grad, weight_grad, bias_grad)


def solution(mesh):
    return jax.shard_map(
        shards,
        mesh=mesh,
        in_specs=(
            P("ch", "sp", None, None),
            P(None, ("sp", "ch"), None),
            P(),
            P(),
            P("ch", "sp", None, None),
        ),
        out_specs=(
            P("ch", "sp", None, None),
            P("ch", "sp", None, None),
            P(None, ("sp", "ch"), None),
            P(),
            P(),
        ),
        check_vma=False,
    )
```

```python
import math

import jax
import jax.numpy as jnp
from jax import lax
from jax.sharding import PartitionSpec as P

KX = 16
KY = 16
KZ = 16
KT = 8
GY = 64
GZ = 64
GT = 32
KYZ = 256
Q = 2048
LANES = 128
SUB = 8


PRECISE = lax.Precision.HIGHEST
SQRT_HALF = 0.7071067811865476
INV_ROOT_TWO_PI = 0.3989422804014327


def wave_table(length, kept_rows, positions):
    row_ids = jnp.arange(kept_rows, dtype=jnp.int32)
    half_kept = kept_rows // 2
    frequency = jnp.where(row_ids <= half_kept, row_ids, row_ids - half_kept)
    phase_ids = frequency[:, None] * positions[None, :] % length
    angles = 2.0 * math.pi / length * phase_ids.astype(jnp.float32)
    waves = jnp.where((row_ids <= half_kept)[:, None], jnp.cos(angles), jnp.sin(angles))
    return math.sqrt(2.0 / length) * waves


def exact_spread(rows, selector):
    total = None
    rest = rows
    for _ in range(3):
        piece = rest.astype(jnp.bfloat16)
        rest = rest - piece.astype(jnp.float32)
        part = jnp.dot(piece, selector, preferred_element_type=jnp.float32)
        total = part if total is None else total + part
    return total


def plane_table():
    wave_y = wave_table(GY, KY, jnp.arange(GY, dtype=jnp.int32))
    wave_z = wave_table(GZ, KZ, jnp.arange(GZ, dtype=jnp.int32))
    y_rows = jnp.repeat(wave_y, KZ, axis=0)
    z_rows = jnp.tile(wave_z, (KY, 1))
    cells = jnp.arange(GY * GZ, dtype=jnp.int32)
    y_rows, z_rows, cells = lax.optimization_barrier((y_rows, z_rows, cells))
    pick_y = (cells[None, :] // GZ == jnp.arange(GY, dtype=jnp.int32)[:, None]).astype(jnp.bfloat16)
    pick_z = (cells[None, :] % GZ == jnp.arange(GZ, dtype=jnp.int32)[:, None]).astype(jnp.bfloat16)
    product = exact_spread(y_rows, pick_y) * exact_spread(z_rows, pick_z)
    return product.astype(jnp.bfloat16)


def split_dot(values, table):
    high = values.astype(jnp.bfloat16)
    low = (values - high.astype(jnp.float32)).astype(jnp.bfloat16)
    return jnp.dot(high, table, preferred_element_type=jnp.float32) + jnp.dot(
        low, table, preferred_element_type=jnp.float32
    )


def to_spectrum(values, yz_table, time_table, x_table, extra=None):
    steps_here, planes, channels, plane_cells = values.shape
    sp_count = lax.axis_size("sp")
    flat = jnp.einsum(
        "qc,rc->qr", yz_table, values.reshape(-1, plane_cells), preferred_element_type=jnp.float32
    ).reshape(KYZ, steps_here, channels)
    partial = jnp.einsum("kt,ptc->kpc", time_table, flat, precision=PRECISE)
    send = partial.reshape(sp_count, SUB, LANES)
    if extra is not None:
        rider = jnp.zeros((sp_count, SUB, LANES), jnp.float32)
        rider = rider.at[:, 0, : Q // sp_count].set(extra.reshape(sp_count, -1))
        send = jnp.concatenate([send, rider], axis=1)
    arrived = lax.all_to_all(send, "sp", 0, 0, tiled=True)
    modes = jnp.einsum("kx,xrl->krl", x_table, arrived[:, :SUB], precision=PRECISE)
    if extra is not None:
        rider_sum = jnp.sum(arrived[:, SUB, : Q // sp_count], axis=0)
        ch_count = lax.axis_size("ch")
        row = jnp.zeros((ch_count, SUB // ch_count, LANES), jnp.float32)
        row = row.at[:, 0, : rider_sum.shape[0] // ch_count].set(rider_sum.reshape(ch_count, -1))
        modes = jnp.concatenate([modes, row.reshape(1, SUB, LANES)], axis=0)
    scattered = lax.psum_scatter(modes, "ch", scatter_dimension=1, tiled=True)
    owned = scattered[:KX].reshape(KX, -1, channels)
    if extra is None:
        return owned
    return owned, scattered[KX, 0, : Q // (sp_count * lax.axis_size("ch"))]


def to_planes(block, x_table, time_table, yz_table, steps_here, extra=None):
    channels = block.shape[2]
    sp_count = lax.axis_size("sp")
    ch_count = lax.axis_size("ch")
    rows = block.reshape(KX, SUB // ch_count, LANES)
    if extra is not None:
        row = jnp.zeros((1, SUB // ch_count, LANES), jnp.float32).at[0, 0, : extra.shape[0]].set(extra)
        rows = jnp.concatenate([rows, row], axis=0)
    gathered = lax.all_gather(rows, "ch", axis=1, tiled=True)
    spread = jnp.einsum("kx,krl->xrl", x_table, gathered[:KX], precision=PRECISE)
    if extra is not None:
        rider = jnp.broadcast_to(gathered[KX][None], (sp_count, SUB, LANES))
        spread = jnp.concatenate([spread, rider], axis=1)
    returned = lax.all_to_all(spread, "sp", 0, 0, tiled=True)
    total = None
    if extra is not None:
        pieces = returned[:, SUB:].reshape(sp_count, ch_count, SUB // ch_count, LANES)
        total = pieces[:, :, 0, : extra.shape[0]].reshape(-1)
    modes = returned[:, :SUB].reshape(KT, KYZ, channels)
    time_spread = jnp.einsum("kt,kpo->top", time_table, modes, precision=PRECISE)
    result = split_dot(time_spread.reshape(-1, KYZ), yz_table)
    return result.reshape(steps_here, 1, channels, -1), total


def shards(field, spectral_weight, point_weight, bias, cotangent):
    steps_here, planes, channels, plane_cells = field.shape
    sp_count = lax.axis_size("sp")
    grid_x = planes * sp_count
    forward_x = wave_table(grid_x, KX, jnp.arange(grid_x, dtype=jnp.int32))
    inverse_x = forward_x * math.sqrt(grid_x / KX)
    time_ids = lax.axis_index("ch") * steps_here + jnp.arange(steps_here, dtype=jnp.int32)
    forward_t = wave_table(GT, KT, time_ids)
    inverse_t = forward_t * math.sqrt(GT / KT)
    inverse_t4 = inverse_t * float(math.sqrt(GY / KY) * math.sqrt(GZ / KZ))
    yz_table = plane_table()
    coeffs = to_spectrum(field, yz_table, forward_t, forward_x)
    weights = spectral_weight.reshape(KX, -1, channels, channels).astype(jnp.float32)
    mixed_modes = jnp.einsum("kqi,kqio->kqo", coeffs, weights, precision=PRECISE)
    spatial, _ = to_planes(mixed_modes, inverse_x, inverse_t4, yz_table, steps_here)
    field_rows = field.reshape(-1, channels, plane_cells)
    linear = jnp.einsum(
        "io,riy->roy", point_weight, field_rows, preferred_element_type=jnp.float32
    ).reshape(spatial.shape)
    preact = spatial + linear + bias[None, None, :, None]
    normal_cdf = 0.5 * (1.0 + lax.erf(preact * SQRT_HALF))
    activated = (preact * normal_cdf).astype(jnp.bfloat16)
    slope = normal_cdf + preact * jnp.exp(-0.5 * preact * preact) * INV_ROOT_TWO_PI
    slopes = (cotangent.astype(jnp.float32) * slope).astype(jnp.bfloat16)
    slope_rows = slopes.reshape(-1, channels, plane_cells)
    weight_part = jnp.einsum("riy,roy->io", field_rows, slope_rows, preferred_element_type=jnp.float32)
    bias_part = jnp.sum(slopes.astype(jnp.float32), axis=(0, 1, 3))
    packed = jnp.concatenate([weight_part.reshape(-1), bias_part])
    packed = jnp.pad(packed, (0, Q - packed.shape[0]))
    slope_modes, packed_part = to_spectrum(slopes, yz_table, inverse_t4, inverse_x, extra=packed)
    spec_scale = math.sqrt(KX * Q / (grid_x * GY * GZ * GT))
    spectral_grad = (spec_scale * jnp.einsum("kqi,kqo->kqio", coeffs, slope_modes)).reshape(
        KX, -1, channels * channels
    )
    coeff_grad = jnp.einsum("kqio,kqo->kqi", weights, slope_modes, precision=PRECISE)
    grad_spatial, packed_sum = to_planes(
        coeff_grad, forward_x, forward_t, yz_table, steps_here, extra=packed_part
    )
    cell_scale = 1.0 / math.sqrt(grid_x * GY * GZ * GT)
    weight_grad = cell_scale * packed_sum[: channels * channels].reshape(channels, channels)
    bias_grad = cell_scale * packed_sum[channels * channels : channels * channels + channels]
    point_part = jnp.einsum(
        "io,roy->riy", point_weight, slope_rows, preferred_element_type=jnp.float32
    ).reshape(grad_spatial.shape)
    field_grad = (grad_spatial + point_part).astype(jnp.bfloat16)
    return (activated, field_grad, spectral_grad, weight_grad, bias_grad)


def solution(mesh):
    return jax.shard_map(
        shards,
        mesh=mesh,
        in_specs=(
            P("ch", "sp", None, None),
            P(None, ("sp", "ch"), None),
            P(),
            P(),
            P("ch", "sp", None, None),
        ),
        out_specs=(
            P("ch", "sp", None, None),
            P("ch", "sp", None, None),
            P(None, ("sp", "ch"), None),
            P(),
            P(),
        ),
        check_vma=False,
    )
```

```python
import math

import jax
import jax.numpy as jnp
from jax import lax
from jax.sharding import PartitionSpec as P

KX = 16
KY = 16
KZ = 16
KT = 8
GY = 64
GZ = 64
GT = 32
KYZ = 256
Q = 2048
LANES = 128
SUB = 8


PRECISE = lax.Precision.HIGHEST
SQRT_HALF = 0.7071067811865476
INV_ROOT_TWO_PI = 0.3989422804014327


def wave_table(length, kept_rows, positions):
    row_ids = jnp.arange(kept_rows, dtype=jnp.int32)
    half_kept = kept_rows // 2
    frequency = jnp.where(row_ids <= half_kept, row_ids, row_ids - half_kept)
    phase_ids = frequency[:, None] * positions[None, :] % length
    angles = 2.0 * math.pi / length * phase_ids.astype(jnp.float32)
    waves = jnp.where((row_ids <= half_kept)[:, None], jnp.cos(angles), jnp.sin(angles))
    return math.sqrt(2.0 / length) * waves


def exact_spread(rows, selector):
    total = None
    rest = rows
    for _ in range(3):
        piece = lax.reduce_precision(rest, exponent_bits=8, mantissa_bits=7)
        rest = rest - piece
        part = jnp.dot(piece.astype(jnp.bfloat16), selector, preferred_element_type=jnp.float32)
        total = part if total is None else total + part
    return total


def plane_table():
    wave_y = wave_table(GY, KY, jnp.arange(GY, dtype=jnp.int32))
    wave_z = wave_table(GZ, KZ, jnp.arange(GZ, dtype=jnp.int32))
    y_rows = jnp.repeat(wave_y, KZ, axis=0)
    z_rows = jnp.tile(wave_z, (KY, 1))
    cells = jnp.arange(GY * GZ, dtype=jnp.int32)
    y_rows, z_rows, cells = lax.optimization_barrier((y_rows, z_rows, cells))
    pick_y = (cells[None, :] // GZ == jnp.arange(GY, dtype=jnp.int32)[:, None]).astype(jnp.bfloat16)
    pick_z = (cells[None, :] % GZ == jnp.arange(GZ, dtype=jnp.int32)[:, None]).astype(jnp.bfloat16)
    product = exact_spread(y_rows, pick_y) * exact_spread(z_rows, pick_z)
    return product.astype(jnp.bfloat16)


def split_dot(values, table):
    high = lax.reduce_precision(values, exponent_bits=8, mantissa_bits=7)
    low = (values - high).astype(jnp.bfloat16)
    return jnp.dot(high.astype(jnp.bfloat16), table, preferred_element_type=jnp.float32) + jnp.dot(
        low, table, preferred_element_type=jnp.float32
    )


def to_spectrum(values, yz_table, time_table, x_table, extra=None):
    steps_here, planes, channels, plane_cells = values.shape
    sp_count = lax.axis_size("sp")
    flat = jnp.einsum(
        "qc,rc->qr", yz_table, values.reshape(-1, plane_cells), preferred_element_type=jnp.float32
    ).reshape(KYZ, steps_here, channels)
    partial = jnp.einsum("kt,ptc->kpc", time_table, flat, precision=PRECISE)
    send = partial.reshape(sp_count, SUB, LANES)
    if extra is not None:
        rider = jnp.zeros((sp_count, SUB, LANES), jnp.float32)
        rider = rider.at[:, 0, : Q // sp_count].set(extra.reshape(sp_count, -1))
        send = jnp.concatenate([send, rider], axis=1)
    arrived = lax.all_to_all(send, "sp", 0, 0, tiled=True)
    modes = jnp.einsum("kx,xrl->krl", x_table, arrived[:, :SUB], precision=PRECISE)
    if extra is not None:
        rider_sum = jnp.sum(arrived[:, SUB, : Q // sp_count], axis=0)
        ch_count = lax.axis_size("ch")
        row = jnp.zeros((ch_count, SUB // ch_count, LANES), jnp.float32)
        row = row.at[:, 0, : rider_sum.shape[0] // ch_count].set(rider_sum.reshape(ch_count, -1))
        modes = jnp.concatenate([modes, row.reshape(1, SUB, LANES)], axis=0)
    scattered = lax.psum_scatter(modes, "ch", scatter_dimension=1, tiled=True)
    owned = scattered[:KX].reshape(KX, -1, channels)
    if extra is None:
        return owned
    return owned, scattered[KX, 0, : Q // (sp_count * lax.axis_size("ch"))]


def to_planes(block, x_table, time_table, yz_table, steps_here, extra=None):
    channels = block.shape[2]
    sp_count = lax.axis_size("sp")
    ch_count = lax.axis_size("ch")
    rows = block.reshape(KX, SUB // ch_count, LANES)
    if extra is not None:
        row = jnp.zeros((1, SUB // ch_count, LANES), jnp.float32).at[0, 0, : extra.shape[0]].set(extra)
        rows = jnp.concatenate([rows, row], axis=0)
    gathered = lax.all_gather(rows, "ch", axis=1, tiled=True)
    spread = jnp.einsum("kx,krl->xrl", x_table, gathered[:KX], precision=PRECISE)
    if extra is not None:
        rider = jnp.broadcast_to(gathered[KX][None], (sp_count, SUB, LANES))
        spread = jnp.concatenate([spread, rider], axis=1)
    returned = lax.all_to_all(spread, "sp", 0, 0, tiled=True)
    total = None
    if extra is not None:
        pieces = returned[:, SUB:].reshape(sp_count, ch_count, SUB // ch_count, LANES)
        total = pieces[:, :, 0, : extra.shape[0]].reshape(-1)
    modes = returned[:, :SUB].reshape(KT, KYZ, channels)
    time_spread = jnp.einsum("kt,kpo->top", time_table, modes, precision=PRECISE)
    result = split_dot(time_spread.reshape(-1, KYZ), yz_table)
    return result.reshape(steps_here, 1, channels, -1), total


def shards(field, spectral_weight, point_weight, bias, cotangent):
    steps_here, planes, channels, plane_cells = field.shape
    sp_count = lax.axis_size("sp")
    grid_x = planes * sp_count
    forward_x = wave_table(grid_x, KX, jnp.arange(grid_x, dtype=jnp.int32))
    inverse_x = forward_x * math.sqrt(grid_x / KX)
    time_ids = lax.axis_index("ch") * steps_here + jnp.arange(steps_here, dtype=jnp.int32)
    forward_t = wave_table(GT, KT, time_ids)
    inverse_t = forward_t * math.sqrt(GT / KT)
    inverse_t4 = inverse_t * float(math.sqrt(GY / KY) * math.sqrt(GZ / KZ))
    yz_table = plane_table()
    coeffs = to_spectrum(field, yz_table, forward_t, forward_x)
    weights = spectral_weight.reshape(KX, -1, channels, channels).astype(jnp.float32)
    mixed_modes = jnp.einsum("kqi,kqio->kqo", coeffs, weights, precision=PRECISE)
    spatial, _ = to_planes(mixed_modes, inverse_x, inverse_t4, yz_table, steps_here)
    field_rows = field.reshape(-1, channels, plane_cells)
    linear = jnp.einsum(
        "io,riy->roy", point_weight, field_rows, preferred_element_type=jnp.float32
    ).reshape(spatial.shape)
    preact = spatial + linear + bias[None, None, :, None]
    normal_cdf = 0.5 * (1.0 + lax.erf(preact * SQRT_HALF))
    activated = (preact * normal_cdf).astype(jnp.bfloat16)
    slope = normal_cdf + preact * jnp.exp(-0.5 * preact * preact) * INV_ROOT_TWO_PI
    slopes = (cotangent.astype(jnp.float32) * slope).astype(jnp.bfloat16)
    slope_rows = slopes.reshape(-1, channels, plane_cells)
    weight_part = jnp.einsum("riy,roy->io", field_rows, slope_rows, preferred_element_type=jnp.float32)
    bias_part = jnp.sum(slopes.astype(jnp.float32), axis=(0, 1, 3))
    packed = jnp.concatenate([weight_part.reshape(-1), bias_part])
    packed = jnp.pad(packed, (0, Q - packed.shape[0]))
    slope_modes, packed_part = to_spectrum(slopes, yz_table, inverse_t4, inverse_x, extra=packed)
    spec_scale = math.sqrt(KX * Q / (grid_x * GY * GZ * GT))
    spectral_grad = (spec_scale * jnp.einsum("kqi,kqo->kqio", coeffs, slope_modes)).reshape(
        KX, -1, channels * channels
    )
    coeff_grad = jnp.einsum("kqio,kqo->kqi", weights, slope_modes, precision=PRECISE)
    grad_spatial, packed_sum = to_planes(
        coeff_grad, forward_x, forward_t, yz_table, steps_here, extra=packed_part
    )
    cell_scale = 1.0 / math.sqrt(grid_x * GY * GZ * GT)
    weight_grad = cell_scale * packed_sum[: channels * channels].reshape(channels, channels)
    bias_grad = cell_scale * packed_sum[channels * channels : channels * channels + channels]
    point_part = jnp.einsum(
        "io,roy->riy", point_weight, slope_rows, preferred_element_type=jnp.float32
    ).reshape(grad_spatial.shape)
    field_grad = (grad_spatial + point_part).astype(jnp.bfloat16)
    return (activated, field_grad, spectral_grad, weight_grad, bias_grad)


def solution(mesh):
    return jax.shard_map(
        shards,
        mesh=mesh,
        in_specs=(
            P("ch", "sp", None, None),
            P(None, ("sp", "ch"), None),
            P(),
            P(),
            P("ch", "sp", None, None),
        ),
        out_specs=(
            P("ch", "sp", None, None),
            P("ch", "sp", None, None),
            P(None, ("sp", "ch"), None),
            P(),
            P(),
        ),
        check_vma=False,
    )
```

```python
import math

import jax
import jax.numpy as jnp
from jax import lax
from jax.sharding import PartitionSpec as P

KX = 16
KY = 16
KZ = 16
KT = 8
GY = 64
GZ = 64
GT = 32
KYZ = 256
Q = 2048
LANES = 128
SUB = 8


PRECISE = lax.Precision.HIGHEST
SQRT_HALF = 0.7071067811865476
INV_ROOT_TWO_PI = 0.3989422804014327


def wave_table(length, kept_rows, positions):
    row_ids = jnp.arange(kept_rows, dtype=jnp.int32)
    half_kept = kept_rows // 2
    frequency = jnp.where(row_ids <= half_kept, row_ids, row_ids - half_kept)
    phase_ids = frequency[:, None] * positions[None, :] % length
    angles = 2.0 * math.pi / length * phase_ids.astype(jnp.float32)
    waves = jnp.where((row_ids <= half_kept)[:, None], jnp.cos(angles), jnp.sin(angles))
    return math.sqrt(2.0 / length) * waves


def exact_spread(rows, selector):
    total = None
    rest = rows
    for _ in range(3):
        piece = lax.reduce_precision(rest, exponent_bits=8, mantissa_bits=7)
        rest = rest - piece
        part = jnp.dot(piece.astype(jnp.bfloat16), selector, preferred_element_type=jnp.float32)
        total = part if total is None else total + part
    return total


def plane_table():
    wave_y = wave_table(GY, KY, jnp.arange(GY, dtype=jnp.int32))
    wave_z = wave_table(GZ, KZ, jnp.arange(GZ, dtype=jnp.int32))
    y_rows = jnp.repeat(wave_y, KZ, axis=0)
    z_rows = jnp.tile(wave_z, (KY, 1))
    cells = jnp.arange(GY * GZ, dtype=jnp.int32)
    y_rows, z_rows, cells = lax.optimization_barrier((y_rows, z_rows, cells))
    pick_y = (cells[None, :] // GZ == jnp.arange(GY, dtype=jnp.int32)[:, None]).astype(jnp.bfloat16)
    pick_z = (cells[None, :] % GZ == jnp.arange(GZ, dtype=jnp.int32)[:, None]).astype(jnp.bfloat16)
    product = exact_spread(y_rows, pick_y) * exact_spread(z_rows, pick_z)
    return product.astype(jnp.bfloat16)


def split_dot(values, table):
    high = lax.reduce_precision(values, exponent_bits=8, mantissa_bits=7)
    low = (values - high).astype(jnp.bfloat16)
    return jnp.dot(high.astype(jnp.bfloat16), table, preferred_element_type=jnp.float32) + jnp.dot(
        low, table, preferred_element_type=jnp.float32
    )


def to_spectrum(values, yz_table, time_table, x_table, extra=None):
    steps_here, planes, channels, plane_cells = values.shape
    sp_count = lax.axis_size("sp")
    flat = jnp.einsum(
        "qc,rc->qr", yz_table, values.reshape(-1, plane_cells), preferred_element_type=jnp.float32
    ).reshape(KYZ, steps_here, channels)
    partial = jnp.einsum("kt,ptc->kpc", time_table, flat, precision=PRECISE)
    send = partial.reshape(sp_count, SUB, LANES)
    if extra is not None:
        rider = jnp.zeros((sp_count, SUB, LANES), jnp.float32)
        rider = rider.at[:, 0, : Q // sp_count].set(extra.reshape(sp_count, -1))
        send = jnp.concatenate([send, rider], axis=1)
    arrived = lax.all_to_all(send, "sp", 0, 0, tiled=True)
    modes = jnp.einsum("kx,xrl->krl", x_table, arrived[:, :SUB], precision=PRECISE)
    if extra is not None:
        rider_sum = jnp.sum(arrived[:, SUB, : Q // sp_count], axis=0)
        ch_count = lax.axis_size("ch")
        row = jnp.zeros((ch_count, SUB // ch_count, LANES), jnp.float32)
        row = row.at[:, 0, : rider_sum.shape[0] // ch_count].set(rider_sum.reshape(ch_count, -1))
        modes = jnp.concatenate([modes, row.reshape(1, SUB, LANES)], axis=0)
    ch_count = lax.axis_size("ch")
    parts = lax.all_to_all(modes, "ch", 1, 0, tiled=True)
    scattered = jnp.sum(parts.reshape(ch_count, -1, SUB // ch_count, LANES), axis=0)
    owned = scattered[:KX].reshape(KX, -1, channels)
    if extra is None:
        return owned
    return owned, scattered[KX, 0, : Q // (sp_count * lax.axis_size("ch"))]


def to_planes(block, x_table, time_table, yz_table, steps_here, extra=None):
    channels = block.shape[2]
    sp_count = lax.axis_size("sp")
    ch_count = lax.axis_size("ch")
    rows = block.reshape(KX, SUB // ch_count, LANES)
    if extra is not None:
        row = jnp.zeros((1, SUB // ch_count, LANES), jnp.float32).at[0, 0, : extra.shape[0]].set(extra)
        rows = jnp.concatenate([rows, row], axis=0)
    copies = jnp.broadcast_to(rows[:, None], (rows.shape[0], ch_count) + rows.shape[1:])
    gathered = lax.all_to_all(copies, "ch", 1, 1, tiled=True).reshape(rows.shape[0], SUB, LANES)
    spread = jnp.einsum("kx,krl->xrl", x_table, gathered[:KX], precision=PRECISE)
    if extra is not None:
        rider = jnp.broadcast_to(gathered[KX][None], (sp_count, SUB, LANES))
        spread = jnp.concatenate([spread, rider], axis=1)
    returned = lax.all_to_all(spread, "sp", 0, 0, tiled=True)
    total = None
    if extra is not None:
        pieces = returned[:, SUB:].reshape(sp_count, ch_count, SUB // ch_count, LANES)
        total = pieces[:, :, 0, : extra.shape[0]].reshape(-1)
    modes = returned[:, :SUB].reshape(KT, KYZ, channels)
    time_spread = jnp.einsum("kt,kpo->top", time_table, modes, precision=PRECISE)
    result = split_dot(time_spread.reshape(-1, KYZ), yz_table)
    return result.reshape(steps_here, 1, channels, -1), total


def shards(field, spectral_weight, point_weight, bias, cotangent):
    steps_here, planes, channels, plane_cells = field.shape
    sp_count = lax.axis_size("sp")
    grid_x = planes * sp_count
    forward_x = wave_table(grid_x, KX, jnp.arange(grid_x, dtype=jnp.int32))
    inverse_x = forward_x * math.sqrt(grid_x / KX)
    time_ids = lax.axis_index("ch") * steps_here + jnp.arange(steps_here, dtype=jnp.int32)
    forward_t = wave_table(GT, KT, time_ids)
    inverse_t = forward_t * math.sqrt(GT / KT)
    inverse_t4 = inverse_t * float(math.sqrt(GY / KY) * math.sqrt(GZ / KZ))
    yz_table = plane_table()
    coeffs = to_spectrum(field, yz_table, forward_t, forward_x)
    weights = spectral_weight.reshape(KX, -1, channels, channels).astype(jnp.float32)
    mixed_modes = jnp.einsum("kqi,kqio->kqo", coeffs, weights, precision=PRECISE)
    spatial, _ = to_planes(mixed_modes, inverse_x, inverse_t4, yz_table, steps_here)
    field_rows = field.reshape(-1, channels, plane_cells)
    linear = jnp.einsum(
        "io,riy->roy", point_weight, field_rows, preferred_element_type=jnp.float32
    ).reshape(spatial.shape)
    preact = spatial + linear + bias[None, None, :, None]
    normal_cdf = 0.5 * (1.0 + lax.erf(preact * SQRT_HALF))
    activated = (preact * normal_cdf).astype(jnp.bfloat16)
    slope = normal_cdf + preact * jnp.exp(-0.5 * preact * preact) * INV_ROOT_TWO_PI
    slopes = (cotangent.astype(jnp.float32) * slope).astype(jnp.bfloat16)
    slope_rows = slopes.reshape(-1, channels, plane_cells)
    weight_part = jnp.einsum("riy,roy->io", field_rows, slope_rows, preferred_element_type=jnp.float32)
    bias_part = jnp.sum(slopes.astype(jnp.float32), axis=(0, 1, 3))
    packed = jnp.concatenate([weight_part.reshape(-1), bias_part])
    packed = jnp.pad(packed, (0, Q - packed.shape[0]))
    slope_modes, packed_part = to_spectrum(slopes, yz_table, inverse_t4, inverse_x, extra=packed)
    spec_scale = math.sqrt(KX * Q / (grid_x * GY * GZ * GT))
    spectral_grad = (spec_scale * jnp.einsum("kqi,kqo->kqio", coeffs, slope_modes)).reshape(
        KX, -1, channels * channels
    )
    coeff_grad = jnp.einsum("kqio,kqo->kqi", weights, slope_modes, precision=PRECISE)
    grad_spatial, packed_sum = to_planes(
        coeff_grad, forward_x, forward_t, yz_table, steps_here, extra=packed_part
    )
    cell_scale = 1.0 / math.sqrt(grid_x * GY * GZ * GT)
    weight_grad = cell_scale * packed_sum[: channels * channels].reshape(channels, channels)
    bias_grad = cell_scale * packed_sum[channels * channels : channels * channels + channels]
    point_part = jnp.einsum(
        "io,roy->riy", point_weight, slope_rows, preferred_element_type=jnp.float32
    ).reshape(grad_spatial.shape)
    field_grad = (grad_spatial + point_part).astype(jnp.bfloat16)
    return (activated, field_grad, spectral_grad, weight_grad, bias_grad)


def solution(mesh):
    return jax.shard_map(
        shards,
        mesh=mesh,
        in_specs=(
            P("ch", "sp", None, None),
            P(None, ("sp", "ch"), None),
            P(),
            P(),
            P("ch", "sp", None, None),
        ),
        out_specs=(
            P("ch", "sp", None, None),
            P("ch", "sp", None, None),
            P(None, ("sp", "ch"), None),
            P(),
            P(),
        ),
        check_vma=False,
    )
```

```python
import math

import jax
import jax.numpy as jnp
from jax import lax
from jax.sharding import PartitionSpec as P

KX = 16
KY = 16
KZ = 16
KT = 8
GY = 64
GZ = 64
GT = 32
KYZ = 256
Q = 2048
LANES = 128
SUB = 8


PRECISE = lax.Precision.HIGHEST
SQRT_HALF = 0.7071067811865476
INV_ROOT_TWO_PI = 0.3989422804014327


def wave_table(length, kept_rows, positions):
    row_ids = jnp.arange(kept_rows, dtype=jnp.int32)
    half_kept = kept_rows // 2
    frequency = jnp.where(row_ids <= half_kept, row_ids, row_ids - half_kept)
    phase_ids = frequency[:, None] * positions[None, :] % length
    angles = 2.0 * math.pi / length * phase_ids.astype(jnp.float32)
    waves = jnp.where((row_ids <= half_kept)[:, None], jnp.cos(angles), jnp.sin(angles))
    return math.sqrt(2.0 / length) * waves


def exact_spread(rows, selector):
    total = None
    rest = rows
    for _ in range(3):
        piece = lax.reduce_precision(rest, exponent_bits=8, mantissa_bits=7)
        rest = rest - piece
        part = jnp.dot(piece.astype(jnp.bfloat16), selector, preferred_element_type=jnp.float32)
        total = part if total is None else total + part
    return total


def plane_table():
    wave_y = wave_table(GY, KY, jnp.arange(GY, dtype=jnp.int32))
    wave_z = wave_table(GZ, KZ, jnp.arange(GZ, dtype=jnp.int32))
    y_rows = jnp.repeat(wave_y, KZ, axis=0)
    z_rows = jnp.tile(wave_z, (KY, 1))
    cells = jnp.arange(GY * GZ, dtype=jnp.int32)
    y_rows, z_rows, cells = lax.optimization_barrier((y_rows, z_rows, cells))
    pick_y = (cells[None, :] // GZ == jnp.arange(GY, dtype=jnp.int32)[:, None]).astype(jnp.bfloat16)
    pick_z = (cells[None, :] % GZ == jnp.arange(GZ, dtype=jnp.int32)[:, None]).astype(jnp.bfloat16)
    product = exact_spread(y_rows, pick_y) * exact_spread(z_rows, pick_z)
    return product.astype(jnp.bfloat16)


def split_dot(values, table):
    high = lax.reduce_precision(values, exponent_bits=8, mantissa_bits=7)
    low = (values - high).astype(jnp.bfloat16)
    return jnp.dot(high.astype(jnp.bfloat16), table, preferred_element_type=jnp.float32) + jnp.dot(
        low, table, preferred_element_type=jnp.float32
    )


def sp_size():
    return lax.axis_size("sa") * lax.axis_size("sb")


def sp_all_to_all(send):
    outer, inner = lax.axis_size("sa"), lax.axis_size("sb")
    blocks = send.reshape((outer, inner) + send.shape[1:])
    blocks = lax.all_to_all(blocks, "sb", 1, 1, tiled=True)
    blocks = lax.all_to_all(blocks, "sa", 0, 0, tiled=True)
    return blocks.reshape(send.shape)


def to_spectrum(values, yz_table, time_table, x_table, extra=None):
    steps_here, planes, channels, plane_cells = values.shape
    sp_count = sp_size()
    flat = jnp.einsum(
        "qc,rc->qr", yz_table, values.reshape(-1, plane_cells), preferred_element_type=jnp.float32
    ).reshape(KYZ, steps_here, channels)
    partial = jnp.einsum("kt,ptc->kpc", time_table, flat, precision=PRECISE)
    send = partial.reshape(sp_count, SUB, LANES)
    if extra is not None:
        rider = jnp.zeros((sp_count, SUB, LANES), jnp.float32)
        rider = rider.at[:, 0, : Q // sp_count].set(extra.reshape(sp_count, -1))
        send = jnp.concatenate([send, rider], axis=1)
    arrived = sp_all_to_all(send)
    modes = jnp.einsum("kx,xrl->krl", x_table, arrived[:, :SUB], precision=PRECISE)
    if extra is not None:
        rider_sum = jnp.sum(arrived[:, SUB, : Q // sp_count], axis=0)
        ch_count = lax.axis_size("ch")
        row = jnp.zeros((ch_count, SUB // ch_count, LANES), jnp.float32)
        row = row.at[:, 0, : rider_sum.shape[0] // ch_count].set(rider_sum.reshape(ch_count, -1))
        modes = jnp.concatenate([modes, row.reshape(1, SUB, LANES)], axis=0)
    ch_count = lax.axis_size("ch")
    parts = lax.all_to_all(modes, "ch", 1, 0, tiled=True)
    scattered = jnp.sum(parts.reshape(ch_count, -1, SUB // ch_count, LANES), axis=0)
    owned = scattered[:KX].reshape(KX, -1, channels)
    if extra is None:
        return owned
    return owned, scattered[KX, 0, : Q // (sp_count * lax.axis_size("ch"))]


def to_planes(block, x_table, time_table, yz_table, steps_here, extra=None):
    channels = block.shape[2]
    sp_count = sp_size()
    ch_count = lax.axis_size("ch")
    rows = block.reshape(KX, SUB // ch_count, LANES)
    if extra is not None:
        row = jnp.zeros((1, SUB // ch_count, LANES), jnp.float32).at[0, 0, : extra.shape[0]].set(extra)
        rows = jnp.concatenate([rows, row], axis=0)
    copies = jnp.broadcast_to(rows[:, None], (rows.shape[0], ch_count) + rows.shape[1:])
    gathered = lax.all_to_all(copies, "ch", 1, 1, tiled=True).reshape(rows.shape[0], SUB, LANES)
    spread = jnp.einsum("kx,krl->xrl", x_table, gathered[:KX], precision=PRECISE)
    if extra is not None:
        rider = jnp.broadcast_to(gathered[KX][None], (sp_count, SUB, LANES))
        spread = jnp.concatenate([spread, rider], axis=1)
    returned = sp_all_to_all(spread)
    total = None
    if extra is not None:
        pieces = returned[:, SUB:].reshape(sp_count, ch_count, SUB // ch_count, LANES)
        total = pieces[:, :, 0, : extra.shape[0]].reshape(-1)
    modes = returned[:, :SUB].reshape(KT, KYZ, channels)
    time_spread = jnp.einsum("kt,kpo->top", time_table, modes, precision=PRECISE)
    result = split_dot(time_spread.reshape(-1, KYZ), yz_table)
    return result.reshape(steps_here, 1, channels, -1), total


def shards(field, spectral_weight, point_weight, bias, cotangent):
    steps_here, planes, channels, plane_cells = field.shape
    sp_count = sp_size()
    grid_x = planes * sp_count
    forward_x = wave_table(grid_x, KX, jnp.arange(grid_x, dtype=jnp.int32))
    inverse_x = forward_x * math.sqrt(grid_x / KX)
    time_ids = lax.axis_index("ch") * steps_here + jnp.arange(steps_here, dtype=jnp.int32)
    forward_t = wave_table(GT, KT, time_ids)
    inverse_t = forward_t * math.sqrt(GT / KT)
    inverse_t4 = inverse_t * float(math.sqrt(GY / KY) * math.sqrt(GZ / KZ))
    yz_table = plane_table()
    coeffs = to_spectrum(field, yz_table, forward_t, forward_x)
    weights = spectral_weight.reshape(KX, -1, channels, channels).astype(jnp.float32)
    mixed_modes = jnp.einsum("kqi,kqio->kqo", coeffs, weights, precision=PRECISE)
    spatial, _ = to_planes(mixed_modes, inverse_x, inverse_t4, yz_table, steps_here)
    field_rows = field.reshape(-1, channels, plane_cells)
    linear = jnp.einsum(
        "io,riy->roy", point_weight, field_rows, preferred_element_type=jnp.float32
    ).reshape(spatial.shape)
    preact = spatial + linear + bias[None, None, :, None]
    normal_cdf = 0.5 * (1.0 + lax.erf(preact * SQRT_HALF))
    activated = (preact * normal_cdf).astype(jnp.bfloat16)
    slope = normal_cdf + preact * jnp.exp(-0.5 * preact * preact) * INV_ROOT_TWO_PI
    slopes = (cotangent.astype(jnp.float32) * slope).astype(jnp.bfloat16)
    slope_rows = slopes.reshape(-1, channels, plane_cells)
    weight_part = jnp.einsum("riy,roy->io", field_rows, slope_rows, preferred_element_type=jnp.float32)
    bias_part = jnp.sum(slopes.astype(jnp.float32), axis=(0, 1, 3))
    packed = jnp.concatenate([weight_part.reshape(-1), bias_part])
    packed = jnp.pad(packed, (0, Q - packed.shape[0]))
    slope_modes, packed_part = to_spectrum(slopes, yz_table, inverse_t4, inverse_x, extra=packed)
    spec_scale = math.sqrt(KX * Q / (grid_x * GY * GZ * GT))
    spectral_grad = (spec_scale * jnp.einsum("kqi,kqo->kqio", coeffs, slope_modes)).reshape(
        KX, -1, channels * channels
    )
    coeff_grad = jnp.einsum("kqio,kqo->kqi", weights, slope_modes, precision=PRECISE)
    grad_spatial, packed_sum = to_planes(
        coeff_grad, forward_x, forward_t, yz_table, steps_here, extra=packed_part
    )
    cell_scale = 1.0 / math.sqrt(grid_x * GY * GZ * GT)
    weight_grad = cell_scale * packed_sum[: channels * channels].reshape(channels, channels)
    bias_grad = cell_scale * packed_sum[channels * channels : channels * channels + channels]
    point_part = jnp.einsum(
        "io,roy->riy", point_weight, slope_rows, preferred_element_type=jnp.float32
    ).reshape(grad_spatial.shape)
    field_grad = (grad_spatial + point_part).astype(jnp.bfloat16)
    return (activated, field_grad, spectral_grad, weight_grad, bias_grad)


def solution(mesh):
    sp_count, ch_count = mesh.devices.shape
    inner = 8 if sp_count % 8 == 0 else 1
    split_mesh = jax.sharding.Mesh(
        mesh.devices.reshape(sp_count // inner, inner, ch_count), ("sa", "sb", "ch")
    )
    sp = ("sa", "sb")
    return jax.shard_map(
        shards,
        mesh=split_mesh,
        in_specs=(
            P("ch", sp, None, None),
            P(None, sp + ("ch",), None),
            P(),
            P(),
            P("ch", sp, None, None),
        ),
        out_specs=(
            P("ch", sp, None, None),
            P("ch", sp, None, None),
            P(None, sp + ("ch",), None),
            P(),
            P(),
        ),
        check_vma=False,
    )
```

```python
import math

import jax
import jax.numpy as jnp
from jax import lax
from jax.sharding import PartitionSpec as P

KX = 16
KY = 16
KZ = 16
KT = 8
GY = 64
GZ = 64
GT = 32
KYZ = 256
Q = 2048
LANES = 128
SUB = 8


PRECISE = lax.Precision.HIGHEST
SQRT_HALF = 0.7071067811865476
INV_ROOT_TWO_PI = 0.3989422804014327


def wave_table(length, kept_rows, positions):
    row_ids = jnp.arange(kept_rows, dtype=jnp.int32)
    half_kept = kept_rows // 2
    frequency = jnp.where(row_ids <= half_kept, row_ids, row_ids - half_kept)
    phase_ids = frequency[:, None] * positions[None, :] % length
    angles = 2.0 * math.pi / length * phase_ids.astype(jnp.float32)
    waves = jnp.where((row_ids <= half_kept)[:, None], jnp.cos(angles), jnp.sin(angles))
    return math.sqrt(2.0 / length) * waves


def exact_spread(rows, selector):
    total = None
    rest = rows
    for _ in range(3):
        piece = lax.reduce_precision(rest, exponent_bits=8, mantissa_bits=7)
        rest = rest - piece
        part = jnp.dot(piece.astype(jnp.bfloat16), selector, preferred_element_type=jnp.float32)
        total = part if total is None else total + part
    return total


def plane_table():
    wave_y = wave_table(GY, KY, jnp.arange(GY, dtype=jnp.int32))
    wave_z = wave_table(GZ, KZ, jnp.arange(GZ, dtype=jnp.int32))
    y_rows = jnp.repeat(wave_y, KZ, axis=0)
    z_rows = jnp.tile(wave_z, (KY, 1))
    cells = jnp.arange(GY * GZ, dtype=jnp.int32)
    y_rows, z_rows, cells = lax.optimization_barrier((y_rows, z_rows, cells))
    pick_y = (cells[None, :] // GZ == jnp.arange(GY, dtype=jnp.int32)[:, None]).astype(jnp.bfloat16)
    pick_z = (cells[None, :] % GZ == jnp.arange(GZ, dtype=jnp.int32)[:, None]).astype(jnp.bfloat16)
    product = exact_spread(y_rows, pick_y) * exact_spread(z_rows, pick_z)
    return product.astype(jnp.bfloat16)


def split_dot(values, table):
    high = lax.reduce_precision(values, exponent_bits=8, mantissa_bits=7)
    low = (values - high).astype(jnp.bfloat16)
    return jnp.dot(high.astype(jnp.bfloat16), table, preferred_element_type=jnp.float32) + jnp.dot(
        low, table, preferred_element_type=jnp.float32
    )


def to_spectrum(values, yz_table, time_table, x_table, extra=None):
    steps_here, planes, channels, plane_cells = values.shape
    sp_count, ch_count = lax.axis_size("sp"), lax.axis_size("ch")
    own = Q // (sp_count * ch_count)
    blocks = KYZ // (ch_count * own)
    rows_per = own * channels // LANES
    flat = jnp.einsum(
        "qc,rc->qr", yz_table, values.reshape(-1, plane_cells), preferred_element_type=jnp.float32
    ).reshape(blocks, ch_count, own, steps_here, channels)
    partial = jnp.einsum("kt,bmqtc->mkbqc", time_table, flat, precision=PRECISE)
    send = partial.reshape(ch_count, sp_count * rows_per, LANES)
    if extra is not None:
        rider = extra.reshape(sp_count, ch_count, own).transpose(1, 0, 2)
        rider = rider.reshape(ch_count, -1, LANES)
        rider = jnp.pad(rider, ((0, 0), (0, SUB - rider.shape[1]), (0, 0)))
        send = jnp.concatenate([send, rider], axis=1)
    summed = jnp.sum(lax.all_to_all(send, "ch", 0, 0, tiled=True), axis=0)
    data = summed[: sp_count * rows_per].reshape(sp_count, rows_per, LANES)
    if extra is not None:
        pieces = summed[sp_count * rows_per :].reshape(-1)[: sp_count * own].reshape(sp_count, own)
        rider = jnp.zeros((sp_count, 1, LANES), jnp.float32).at[:, 0, :own].set(pieces)
        data = jnp.concatenate([data, rider], axis=1)
    arrived = lax.all_to_all(data, "sp", 0, 0, tiled=True)
    owned = jnp.einsum("kx,xrl->krl", x_table, arrived[:, :rows_per], precision=PRECISE)
    owned = owned.reshape(KX, own, channels)
    if extra is None:
        return owned
    return owned, jnp.sum(arrived[:, rows_per, :own], axis=0)


def to_planes(block, x_table, time_table, yz_table, steps_here, extra=None):
    channels = block.shape[2]
    sp_count, ch_count = lax.axis_size("sp"), lax.axis_size("ch")
    own = block.shape[1]
    blocks = KYZ // (ch_count * own)
    rows_per = own * channels // LANES
    rows = block.reshape(KX, rows_per, LANES)
    spread = jnp.einsum("kx,krl->xrl", x_table, rows, precision=PRECISE)
    if extra is not None:
        rider = jnp.zeros((sp_count, 1, LANES), jnp.float32).at[:, 0, :own].set(
            jnp.broadcast_to(extra[None], (sp_count, own))
        )
        spread = jnp.concatenate([spread, rider], axis=1)
    returned = lax.all_to_all(spread, "sp", 0, 0, tiled=True)
    local = returned[:, :rows_per].reshape(sp_count * rows_per, LANES)
    if extra is not None:
        pieces = returned[:, rows_per, :own].reshape(-1, LANES)
        pieces = jnp.pad(pieces, ((0, SUB - pieces.shape[0]), (0, 0)))
        local = jnp.concatenate([local, pieces], axis=0)
    copies = jnp.broadcast_to(local[None], (ch_count,) + local.shape)
    gathered = lax.all_to_all(copies, "ch", 0, 0, tiled=True)
    total = None
    if extra is not None:
        tail = gathered[:, sp_count * rows_per :].reshape(ch_count, -1)[:, : sp_count * own]
        total = tail.reshape(ch_count, sp_count, own).transpose(1, 0, 2).reshape(-1)
    modes = gathered[:, : sp_count * rows_per].reshape(ch_count, KT, blocks, own, channels)
    time_spread = jnp.einsum("kt,mkbqo->tobmq", time_table, modes, precision=PRECISE)
    result = split_dot(time_spread.reshape(-1, KYZ), yz_table)
    return result.reshape(steps_here, 1, channels, -1), total


def shards(field, spectral_weight, point_weight, bias, cotangent):
    steps_here, planes, channels, plane_cells = field.shape
    sp_count = lax.axis_size("sp")
    grid_x = planes * sp_count
    forward_x = wave_table(grid_x, KX, jnp.arange(grid_x, dtype=jnp.int32))
    inverse_x = forward_x * math.sqrt(grid_x / KX)
    time_ids = lax.axis_index("ch") * steps_here + jnp.arange(steps_here, dtype=jnp.int32)
    forward_t = wave_table(GT, KT, time_ids)
    inverse_t = forward_t * math.sqrt(GT / KT)
    inverse_t4 = inverse_t * float(math.sqrt(GY / KY) * math.sqrt(GZ / KZ))
    yz_table = plane_table()
    coeffs = to_spectrum(field, yz_table, forward_t, forward_x)
    weights = spectral_weight.reshape(KX, -1, channels, channels).astype(jnp.float32)
    mixed_modes = jnp.einsum("kqi,kqio->kqo", coeffs, weights, precision=PRECISE)
    spatial, _ = to_planes(mixed_modes, inverse_x, inverse_t4, yz_table, steps_here)
    field_rows = field.reshape(-1, channels, plane_cells)
    linear = jnp.einsum(
        "io,riy->roy", point_weight, field_rows, preferred_element_type=jnp.float32
    ).reshape(spatial.shape)
    preact = spatial + linear + bias[None, None, :, None]
    normal_cdf = 0.5 * (1.0 + lax.erf(preact * SQRT_HALF))
    activated = (preact * normal_cdf).astype(jnp.bfloat16)
    slope = normal_cdf + preact * jnp.exp(-0.5 * preact * preact) * INV_ROOT_TWO_PI
    slopes = (cotangent.astype(jnp.float32) * slope).astype(jnp.bfloat16)
    slope_rows = slopes.reshape(-1, channels, plane_cells)
    weight_part = jnp.einsum("riy,roy->io", field_rows, slope_rows, preferred_element_type=jnp.float32)
    bias_part = jnp.sum(slopes.astype(jnp.float32), axis=(0, 1, 3))
    packed = jnp.concatenate([weight_part.reshape(-1), bias_part])
    packed = jnp.pad(packed, (0, Q - packed.shape[0]))
    slope_modes, packed_part = to_spectrum(slopes, yz_table, inverse_t4, inverse_x, extra=packed)
    spec_scale = math.sqrt(KX * Q / (grid_x * GY * GZ * GT))
    spectral_grad = (spec_scale * jnp.einsum("kqi,kqo->kqio", coeffs, slope_modes)).reshape(
        KX, -1, channels * channels
    )
    coeff_grad = jnp.einsum("kqio,kqo->kqi", weights, slope_modes, precision=PRECISE)
    grad_spatial, packed_sum = to_planes(
        coeff_grad, forward_x, forward_t, yz_table, steps_here, extra=packed_part
    )
    cell_scale = 1.0 / math.sqrt(grid_x * GY * GZ * GT)
    weight_grad = cell_scale * packed_sum[: channels * channels].reshape(channels, channels)
    bias_grad = cell_scale * packed_sum[channels * channels : channels * channels + channels]
    point_part = jnp.einsum(
        "io,roy->riy", point_weight, slope_rows, preferred_element_type=jnp.float32
    ).reshape(grad_spatial.shape)
    field_grad = (grad_spatial + point_part).astype(jnp.bfloat16)
    return (activated, field_grad, spectral_grad, weight_grad, bias_grad)


def solution(mesh):
    return jax.shard_map(
        shards,
        mesh=mesh,
        in_specs=(
            P("ch", "sp", None, None),
            P(None, ("sp", "ch"), None),
            P(),
            P(),
            P("ch", "sp", None, None),
        ),
        out_specs=(
            P("ch", "sp", None, None),
            P("ch", "sp", None, None),
            P(None, ("sp", "ch"), None),
            P(),
            P(),
        ),
        check_vma=False,
    )
```

```python
import math

import jax
import jax.numpy as jnp
from jax import lax
from jax.sharding import PartitionSpec as P

KX = 16
KY = 16
KZ = 16
KT = 8
GY = 64
GZ = 64
GT = 32
KYZ = 256
Q = 2048
LANES = 128
SUB = 8


PRECISE = lax.Precision.HIGHEST
SQRT_HALF = 0.7071067811865476
INV_ROOT_TWO_PI = 0.3989422804014327


def wave_table(length, kept_rows, positions):
    row_ids = jnp.arange(kept_rows, dtype=jnp.int32)
    half_kept = kept_rows // 2
    frequency = jnp.where(row_ids <= half_kept, row_ids, row_ids - half_kept)
    phase_ids = frequency[:, None] * positions[None, :] % length
    angles = 2.0 * math.pi / length * phase_ids.astype(jnp.float32)
    waves = jnp.where((row_ids <= half_kept)[:, None], jnp.cos(angles), jnp.sin(angles))
    return math.sqrt(2.0 / length) * waves


def exact_spread(rows, selector):
    pieces = []
    rest = rows
    for _ in range(3):
        piece = lax.reduce_precision(rest, exponent_bits=8, mantissa_bits=7)
        rest = rest - piece
        pieces.append(piece.astype(jnp.bfloat16))
    stacked = jnp.concatenate([selector] * 3, axis=0)
    return jnp.dot(jnp.concatenate(pieces, axis=1), stacked, preferred_element_type=jnp.float32)


def plane_table():
    wave_y = wave_table(GY, KY, jnp.arange(GY, dtype=jnp.int32))
    wave_z = wave_table(GZ, KZ, jnp.arange(GZ, dtype=jnp.int32))
    y_rows = jnp.repeat(wave_y, KZ, axis=0)
    z_rows = jnp.tile(wave_z, (KY, 1))
    cells = jnp.arange(GY * GZ, dtype=jnp.int32)
    y_rows, z_rows, cells = lax.optimization_barrier((y_rows, z_rows, cells))
    pick_y = (cells[None, :] // GZ == jnp.arange(GY, dtype=jnp.int32)[:, None]).astype(jnp.bfloat16)
    pick_z = (cells[None, :] % GZ == jnp.arange(GZ, dtype=jnp.int32)[:, None]).astype(jnp.bfloat16)
    product = exact_spread(y_rows, pick_y) * exact_spread(z_rows, pick_z)
    return product.astype(jnp.bfloat16)


def split_dot(values, table):
    high = lax.reduce_precision(values, exponent_bits=8, mantissa_bits=7)
    low = (values - high).astype(jnp.bfloat16)
    return jnp.dot(high.astype(jnp.bfloat16), table, preferred_element_type=jnp.float32) + jnp.dot(
        low, table, preferred_element_type=jnp.float32
    )


def to_spectrum(values, yz_table, time_table, x_table, extra=None):
    steps_here, planes, channels, plane_cells = values.shape
    sp_count, ch_count = lax.axis_size("sp"), lax.axis_size("ch")
    own = Q // (sp_count * ch_count)
    blocks = KYZ // (ch_count * own)
    rows_per = own * channels // LANES
    flat = jnp.einsum(
        "qc,rc->qr", yz_table, values.reshape(-1, plane_cells), preferred_element_type=jnp.float32
    ).reshape(blocks, ch_count, own, steps_here, channels)
    partial = jnp.einsum("kt,bmqtc->mkbqc", time_table, flat, precision=PRECISE)
    send = partial.reshape(ch_count, sp_count * rows_per, LANES)
    if extra is not None:
        rider = extra.reshape(sp_count, ch_count, own).transpose(1, 0, 2)
        rider = rider.reshape(ch_count, -1, LANES)
        rider = jnp.pad(rider, ((0, 0), (0, SUB - rider.shape[1]), (0, 0)))
        send = jnp.concatenate([send, rider], axis=1)
    summed = jnp.sum(lax.all_to_all(send, "ch", 0, 0, tiled=True), axis=0)
    data = summed[: sp_count * rows_per].reshape(sp_count, rows_per, LANES)
    if extra is not None:
        pieces = summed[sp_count * rows_per :].reshape(-1)[: sp_count * own].reshape(sp_count, own)
        rider = jnp.zeros((sp_count, 1, LANES), jnp.float32).at[:, 0, :own].set(pieces)
        data = jnp.concatenate([data, rider], axis=1)
    arrived = lax.all_to_all(data, "sp", 0, 0, tiled=True)
    owned = jnp.einsum("kx,xrl->krl", x_table, arrived[:, :rows_per], precision=PRECISE)
    owned = owned.reshape(KX, own, channels)
    if extra is None:
        return owned
    return owned, jnp.sum(arrived[:, rows_per, :own], axis=0)


def to_planes(block, x_table, time_table, yz_table, steps_here, extra=None):
    channels = block.shape[2]
    sp_count, ch_count = lax.axis_size("sp"), lax.axis_size("ch")
    own = block.shape[1]
    blocks = KYZ // (ch_count * own)
    rows_per = own * channels // LANES
    rows = block.reshape(KX, rows_per, LANES)
    spread = jnp.einsum("kx,krl->xrl", x_table, rows, precision=PRECISE)
    if extra is not None:
        rider = jnp.zeros((sp_count, 1, LANES), jnp.float32).at[:, 0, :own].set(
            jnp.broadcast_to(extra[None], (sp_count, own))
        )
        spread = jnp.concatenate([spread, rider], axis=1)
    returned = lax.all_to_all(spread, "sp", 0, 0, tiled=True)
    local = returned[:, :rows_per].reshape(sp_count * rows_per, LANES)
    if extra is not None:
        pieces = returned[:, rows_per, :own].reshape(-1, LANES)
        pieces = jnp.pad(pieces, ((0, SUB - pieces.shape[0]), (0, 0)))
        local = jnp.concatenate([local, pieces], axis=0)
    copies = jnp.broadcast_to(local[None], (ch_count,) + local.shape)
    gathered = lax.all_to_all(copies, "ch", 0, 0, tiled=True)
    total = None
    if extra is not None:
        tail = gathered[:, sp_count * rows_per :].reshape(ch_count, -1)[:, : sp_count * own]
        total = tail.reshape(ch_count, sp_count, own).transpose(1, 0, 2).reshape(-1)
    modes = gathered[:, : sp_count * rows_per].reshape(ch_count, KT, blocks, own, channels)
    time_spread = jnp.einsum("kt,mkbqo->tobmq", time_table, modes, precision=PRECISE)
    result = split_dot(time_spread.reshape(-1, KYZ), yz_table)
    return result.reshape(steps_here, 1, channels, -1), total


def shards(field, spectral_weight, point_weight, bias, cotangent):
    steps_here, planes, channels, plane_cells = field.shape
    sp_count = lax.axis_size("sp")
    grid_x = planes * sp_count
    forward_x = wave_table(grid_x, KX, jnp.arange(grid_x, dtype=jnp.int32))
    inverse_x = forward_x * math.sqrt(grid_x / KX)
    time_ids = lax.axis_index("ch") * steps_here + jnp.arange(steps_here, dtype=jnp.int32)
    forward_t = wave_table(GT, KT, time_ids)
    inverse_t = forward_t * math.sqrt(GT / KT)
    inverse_t4 = inverse_t * float(math.sqrt(GY / KY) * math.sqrt(GZ / KZ))
    yz_table = plane_table()
    coeffs = to_spectrum(field, yz_table, forward_t, forward_x)
    weights = spectral_weight.reshape(KX, -1, channels, channels).astype(jnp.float32)
    mixed_modes = jnp.einsum("kqi,kqio->kqo", coeffs, weights, precision=PRECISE)
    spatial, _ = to_planes(mixed_modes, inverse_x, inverse_t4, yz_table, steps_here)
    field_rows = field.reshape(-1, channels, plane_cells)
    linear = jnp.einsum(
        "io,riy->roy", point_weight, field_rows, preferred_element_type=jnp.float32
    ).reshape(spatial.shape)
    preact = spatial + linear + bias[None, None, :, None]
    normal_cdf = 0.5 * (1.0 + lax.erf(preact * SQRT_HALF))
    activated = (preact * normal_cdf).astype(jnp.bfloat16)
    slope = normal_cdf + preact * jnp.exp(-0.5 * preact * preact) * INV_ROOT_TWO_PI
    slopes = (cotangent.astype(jnp.float32) * slope).astype(jnp.bfloat16)
    slope_rows = slopes.reshape(-1, channels, plane_cells)
    weight_part = jnp.einsum("riy,roy->io", field_rows, slope_rows, preferred_element_type=jnp.float32)
    bias_part = jnp.sum(slopes.astype(jnp.float32), axis=(0, 1, 3))
    packed = jnp.concatenate([weight_part.reshape(-1), bias_part])
    packed = jnp.pad(packed, (0, Q - packed.shape[0]))
    slope_modes, packed_part = to_spectrum(slopes, yz_table, inverse_t4, inverse_x, extra=packed)
    spec_scale = math.sqrt(KX * Q / (grid_x * GY * GZ * GT))
    spectral_grad = (spec_scale * jnp.einsum("kqi,kqo->kqio", coeffs, slope_modes)).reshape(
        KX, -1, channels * channels
    )
    coeff_grad = jnp.einsum("kqio,kqo->kqi", weights, slope_modes, precision=PRECISE)
    grad_spatial, packed_sum = to_planes(
        coeff_grad, forward_x, forward_t, yz_table, steps_here, extra=packed_part
    )
    cell_scale = 1.0 / math.sqrt(grid_x * GY * GZ * GT)
    weight_grad = cell_scale * packed_sum[: channels * channels].reshape(channels, channels)
    bias_grad = cell_scale * packed_sum[channels * channels : channels * channels + channels]
    point_part = jnp.einsum(
        "io,roy->riy", point_weight, slope_rows, preferred_element_type=jnp.float32
    ).reshape(grad_spatial.shape)
    field_grad = (grad_spatial + point_part).astype(jnp.bfloat16)
    return (activated, field_grad, spectral_grad, weight_grad, bias_grad)


def solution(mesh):
    return jax.shard_map(
        shards,
        mesh=mesh,
        in_specs=(
            P("ch", "sp", None, None),
            P(None, ("sp", "ch"), None),
            P(),
            P(),
            P("ch", "sp", None, None),
        ),
        out_specs=(
            P("ch", "sp", None, None),
            P("ch", "sp", None, None),
            P(None, ("sp", "ch"), None),
            P(),
            P(),
        ),
        check_vma=False,
    )
```

```python
import math

import jax
import jax.numpy as jnp
from jax import lax
from jax.sharding import PartitionSpec as P

KX = 16
KY = 16
KZ = 16
KT = 8
GY = 64
GZ = 64
GT = 32
KYZ = 256
Q = 2048
LANES = 128
SUB = 8


PRECISE = lax.Precision.HIGHEST
SQRT_HALF = 0.7071067811865476
INV_ROOT_TWO_PI = 0.3989422804014327


def wave_table(length, kept_rows, positions):
    row_ids = jnp.arange(kept_rows, dtype=jnp.int32)
    half_kept = kept_rows // 2
    frequency = jnp.where(row_ids <= half_kept, row_ids, row_ids - half_kept)
    phase_ids = frequency[:, None] * positions[None, :] % length
    angles = 2.0 * math.pi / length * phase_ids.astype(jnp.float32)
    waves = jnp.where((row_ids <= half_kept)[:, None], jnp.cos(angles), jnp.sin(angles))
    return math.sqrt(2.0 / length) * waves


def exact_spread(rows, selector):
    pieces = []
    rest = rows
    for _ in range(3):
        piece = lax.reduce_precision(rest, exponent_bits=8, mantissa_bits=7)
        rest = rest - piece
        pieces.append(piece.astype(jnp.bfloat16))
    stacked = jnp.concatenate([selector] * 3, axis=0)
    return jnp.dot(jnp.concatenate(pieces, axis=1), stacked, preferred_element_type=jnp.float32)


def plane_table():
    wave_y = wave_table(GY, KY, jnp.arange(GY, dtype=jnp.int32))
    wave_z = wave_table(GZ, KZ, jnp.arange(GZ, dtype=jnp.int32))
    y_rows = jnp.repeat(wave_y, KZ, axis=0)
    z_rows = jnp.tile(wave_z, (KY, 1))
    cells = jnp.arange(GY * GZ, dtype=jnp.int32)
    y_rows, z_rows, cells = lax.optimization_barrier((y_rows, z_rows, cells))
    pick_y = (cells[None, :] // GZ == jnp.arange(GY, dtype=jnp.int32)[:, None]).astype(jnp.bfloat16)
    pick_z = (cells[None, :] % GZ == jnp.arange(GZ, dtype=jnp.int32)[:, None]).astype(jnp.bfloat16)
    product = exact_spread(y_rows, pick_y) * exact_spread(z_rows, pick_z)
    return product.astype(jnp.bfloat16)


def split_dot(values, table):
    high = lax.reduce_precision(values, exponent_bits=8, mantissa_bits=7)
    low = (values - high).astype(jnp.bfloat16)
    return jnp.dot(high.astype(jnp.bfloat16), table, preferred_element_type=jnp.float32) + jnp.dot(
        low, table, preferred_element_type=jnp.float32
    )


def to_spectrum(values, yz_table, time_table, x_table, extra=None):
    steps_here, planes, channels, plane_cells = values.shape
    sp_count, ch_count = lax.axis_size("sp"), lax.axis_size("ch")
    own = Q // (sp_count * ch_count)
    rows_per = own * channels // LANES
    flat = jnp.einsum(
        "qc,rc->qr", yz_table, values.reshape(-1, plane_cells), preferred_element_type=jnp.float32
    ).reshape(KYZ, steps_here, channels)
    partial = jnp.einsum("kt,ptc->kpc", time_table, flat, precision=PRECISE)
    send = partial.reshape(sp_count * ch_count, rows_per, LANES)
    if extra is not None:
        rider = jnp.zeros((sp_count * ch_count, 1, LANES), jnp.float32)
        rider = rider.at[:, 0, :own].set(extra.reshape(-1, own))
        send = jnp.concatenate([send, rider], axis=1)
    arrived = lax.all_to_all(send, ("sp", "ch"), 0, 0, tiled=True)
    by_plane = arrived[:, :rows_per].reshape(sp_count, ch_count, rows_per, LANES)
    owned = jnp.einsum("kx,xmrl->krl", x_table, by_plane, precision=PRECISE)
    owned = owned.reshape(KX, own, channels)
    if extra is None:
        return owned
    return owned, jnp.sum(arrived[:, rows_per, :own], axis=0)


def to_planes(block, x_table, time_table, yz_table, steps_here, extra=None):
    channels = block.shape[2]
    sp_count, ch_count = lax.axis_size("sp"), lax.axis_size("ch")
    own = block.shape[1]
    rows_per = own * channels // LANES
    rows = block.reshape(KX, rows_per, LANES)
    spread = jnp.einsum("kx,krl->xrl", x_table, rows, precision=PRECISE)
    if extra is not None:
        rider = jnp.zeros((sp_count, 1, LANES), jnp.float32).at[:, 0, :own].set(
            jnp.broadcast_to(extra[None], (sp_count, own))
        )
        spread = jnp.concatenate([spread, rider], axis=1)
    copies = jnp.broadcast_to(spread[:, None], (sp_count, ch_count) + spread.shape[1:])
    returned = lax.all_to_all(
        copies.reshape((-1,) + spread.shape[1:]), ("sp", "ch"), 0, 0, tiled=True
    )
    total = returned[:, rows_per, :own].reshape(-1) if extra is not None else None
    modes = returned[:, :rows_per].reshape(KT, KYZ, channels)
    time_spread = jnp.einsum("kt,kpo->top", time_table, modes, precision=PRECISE)
    result = split_dot(time_spread.reshape(-1, KYZ), yz_table)
    return result.reshape(steps_here, 1, channels, -1), total


def shards(field, spectral_weight, point_weight, bias, cotangent):
    steps_here, planes, channels, plane_cells = field.shape
    sp_count = lax.axis_size("sp")
    grid_x = planes * sp_count
    forward_x = wave_table(grid_x, KX, jnp.arange(grid_x, dtype=jnp.int32))
    inverse_x = forward_x * math.sqrt(grid_x / KX)
    time_ids = lax.axis_index("ch") * steps_here + jnp.arange(steps_here, dtype=jnp.int32)
    forward_t = wave_table(GT, KT, time_ids)
    inverse_t = forward_t * math.sqrt(GT / KT)
    inverse_t4 = inverse_t * float(math.sqrt(GY / KY) * math.sqrt(GZ / KZ))
    yz_table = plane_table()
    coeffs = to_spectrum(field, yz_table, forward_t, forward_x)
    weights = spectral_weight.reshape(KX, -1, channels, channels).astype(jnp.float32)
    mixed_modes = jnp.einsum("kqi,kqio->kqo", coeffs, weights, precision=PRECISE)
    spatial, _ = to_planes(mixed_modes, inverse_x, inverse_t4, yz_table, steps_here)
    field_rows = field.reshape(-1, channels, plane_cells)
    linear = jnp.einsum(
        "io,riy->roy", point_weight, field_rows, preferred_element_type=jnp.float32
    ).reshape(spatial.shape)
    preact = spatial + linear + bias[None, None, :, None]
    normal_cdf = 0.5 * (1.0 + lax.erf(preact * SQRT_HALF))
    activated = (preact * normal_cdf).astype(jnp.bfloat16)
    slope = normal_cdf + preact * jnp.exp(-0.5 * preact * preact) * INV_ROOT_TWO_PI
    slopes = (cotangent.astype(jnp.float32) * slope).astype(jnp.bfloat16)
    slope_rows = slopes.reshape(-1, channels, plane_cells)
    weight_part = jnp.einsum("riy,roy->io", field_rows, slope_rows, preferred_element_type=jnp.float32)
    bias_part = jnp.sum(slopes.astype(jnp.float32), axis=(0, 1, 3))
    packed = jnp.concatenate([weight_part.reshape(-1), bias_part])
    packed = jnp.pad(packed, (0, Q - packed.shape[0]))
    slope_modes, packed_part = to_spectrum(slopes, yz_table, inverse_t4, inverse_x, extra=packed)
    spec_scale = math.sqrt(KX * Q / (grid_x * GY * GZ * GT))
    spectral_grad = (spec_scale * jnp.einsum("kqi,kqo->kqio", coeffs, slope_modes)).reshape(
        KX, -1, channels * channels
    )
    coeff_grad = jnp.einsum("kqio,kqo->kqi", weights, slope_modes, precision=PRECISE)
    grad_spatial, packed_sum = to_planes(
        coeff_grad, forward_x, forward_t, yz_table, steps_here, extra=packed_part
    )
    cell_scale = 1.0 / math.sqrt(grid_x * GY * GZ * GT)
    weight_grad = cell_scale * packed_sum[: channels * channels].reshape(channels, channels)
    bias_grad = cell_scale * packed_sum[channels * channels : channels * channels + channels]
    point_part = jnp.einsum(
        "io,roy->riy", point_weight, slope_rows, preferred_element_type=jnp.float32
    ).reshape(grad_spatial.shape)
    field_grad = (grad_spatial + point_part).astype(jnp.bfloat16)
    return (activated, field_grad, spectral_grad, weight_grad, bias_grad)


def solution(mesh):
    return jax.shard_map(
        shards,
        mesh=mesh,
        in_specs=(
            P("ch", "sp", None, None),
            P(None, ("sp", "ch"), None),
            P(),
            P(),
            P("ch", "sp", None, None),
        ),
        out_specs=(
            P("ch", "sp", None, None),
            P("ch", "sp", None, None),
            P(None, ("sp", "ch"), None),
            P(),
            P(),
        ),
        check_vma=False,
    )
```

```python
import math

import jax
import jax.numpy as jnp
from jax import lax
from jax.sharding import PartitionSpec as P

KX = 16
KY = 16
KZ = 16
KT = 8
GY = 64
GZ = 64
GT = 32
KYZ = 256
Q = 2048
LANES = 128
SUB = 8


PRECISE = lax.Precision.HIGHEST
SQRT_HALF = 0.7071067811865476
INV_ROOT_TWO_PI = 0.3989422804014327


def wave_table(length, kept_rows, positions):
    row_ids = jnp.arange(kept_rows, dtype=jnp.int32)
    half_kept = kept_rows // 2
    frequency = jnp.where(row_ids <= half_kept, row_ids, row_ids - half_kept)
    phase_ids = frequency[:, None] * positions[None, :] % length
    angles = 2.0 * math.pi / length * phase_ids.astype(jnp.float32)
    waves = jnp.where((row_ids <= half_kept)[:, None], jnp.cos(angles), jnp.sin(angles))
    return math.sqrt(2.0 / length) * waves


def exact_spread(rows, selector):
    pieces = []
    rest = rows
    for _ in range(3):
        piece = lax.reduce_precision(rest, exponent_bits=8, mantissa_bits=7)
        rest = rest - piece
        pieces.append(piece.astype(jnp.bfloat16))
    stacked = jnp.concatenate([selector] * 3, axis=0)
    return jnp.dot(jnp.concatenate(pieces, axis=1), stacked, preferred_element_type=jnp.float32)


def plane_table():
    wave_y = wave_table(GY, KY, jnp.arange(GY, dtype=jnp.int32))
    wave_z = wave_table(GZ, KZ, jnp.arange(GZ, dtype=jnp.int32))
    y_rows = jnp.repeat(wave_y, KZ, axis=0)
    z_rows = jnp.tile(wave_z, (KY, 1))
    cells = jnp.arange(GY * GZ, dtype=jnp.int32)
    y_rows, z_rows, cells = lax.optimization_barrier((y_rows, z_rows, cells))
    pick_y = (cells[None, :] // GZ == jnp.arange(GY, dtype=jnp.int32)[:, None]).astype(jnp.bfloat16)
    pick_z = (cells[None, :] % GZ == jnp.arange(GZ, dtype=jnp.int32)[:, None]).astype(jnp.bfloat16)
    product = exact_spread(y_rows, pick_y) * exact_spread(z_rows, pick_z)
    return product.astype(jnp.bfloat16)


def split_dot(values, table):
    high = lax.reduce_precision(values, exponent_bits=8, mantissa_bits=7)
    low = (values - high).astype(jnp.bfloat16)
    return jnp.dot(high.astype(jnp.bfloat16), table, preferred_element_type=jnp.float32) + jnp.dot(
        low, table, preferred_element_type=jnp.float32
    )


def to_spectrum(values, yz_table, time_table, x_table, extra=None):
    steps_here, planes, channels, plane_cells = values.shape
    sp_count, ch_count = lax.axis_size("sp"), lax.axis_size("ch")
    own = Q // (sp_count * ch_count)
    rows_per = own * channels // LANES
    flat = jnp.einsum(
        "qc,rc->qr", yz_table, values.reshape(-1, plane_cells), preferred_element_type=jnp.float32
    ).reshape(KYZ, steps_here, channels)
    partial = jnp.einsum("kt,ptc->kpc", time_table, flat, precision=PRECISE)
    send = partial.reshape(sp_count * ch_count, rows_per, LANES)
    if extra is not None:
        rider = jnp.zeros((sp_count * ch_count, 1, LANES), jnp.float32)
        rider = rider.at[:, 0, :own].set(extra.reshape(-1, own))
        send = jnp.concatenate([send, rider], axis=1)
    arrived = lax.all_to_all(send, ("sp", "ch"), 0, 0, tiled=True)
    by_plane = arrived[:, :rows_per].reshape(sp_count, ch_count, rows_per, LANES)
    owned = jnp.einsum("kx,xmrl->krl", x_table, by_plane, precision=PRECISE)
    owned = owned.reshape(KX, own, channels)
    if extra is None:
        return owned
    return owned, jnp.sum(arrived[:, rows_per, :own], axis=0)


def to_planes(block, x_table, time_table, yz_table, steps_here, extra=None, one_pass=False):
    channels = block.shape[2]
    sp_count, ch_count = lax.axis_size("sp"), lax.axis_size("ch")
    own = block.shape[1]
    rows_per = own * channels // LANES
    rows = block.reshape(KX, rows_per, LANES)
    spread = jnp.einsum("kx,krl->xrl", x_table, rows, precision=PRECISE)
    if extra is not None:
        rider = jnp.zeros((sp_count, 1, LANES), jnp.float32).at[:, 0, :own].set(
            jnp.broadcast_to(extra[None], (sp_count, own))
        )
        spread = jnp.concatenate([spread, rider], axis=1)
    copies = jnp.broadcast_to(spread[:, None], (sp_count, ch_count) + spread.shape[1:])
    returned = lax.all_to_all(
        copies.reshape((-1,) + spread.shape[1:]), ("sp", "ch"), 0, 0, tiled=True
    )
    total = returned[:, rows_per, :own].reshape(-1) if extra is not None else None
    modes = returned[:, :rows_per].reshape(KT, KYZ, channels)
    time_spread = jnp.einsum("kt,kpo->top", time_table, modes, precision=PRECISE)
    time_spread = time_spread.reshape(-1, KYZ)
    if one_pass:
        result = jnp.dot(time_spread.astype(jnp.bfloat16), yz_table, preferred_element_type=jnp.float32)
    else:
        result = split_dot(time_spread, yz_table)
    return result.reshape(steps_here, 1, channels, -1), total


def shards(field, spectral_weight, point_weight, bias, cotangent):
    steps_here, planes, channels, plane_cells = field.shape
    sp_count = lax.axis_size("sp")
    grid_x = planes * sp_count
    forward_x = wave_table(grid_x, KX, jnp.arange(grid_x, dtype=jnp.int32))
    inverse_x = forward_x * math.sqrt(grid_x / KX)
    time_ids = lax.axis_index("ch") * steps_here + jnp.arange(steps_here, dtype=jnp.int32)
    forward_t = wave_table(GT, KT, time_ids)
    inverse_t = forward_t * math.sqrt(GT / KT)
    inverse_t4 = inverse_t * float(math.sqrt(GY / KY) * math.sqrt(GZ / KZ))
    yz_table = plane_table()
    coeffs = to_spectrum(field, yz_table, forward_t, forward_x)
    weights = spectral_weight.reshape(KX, -1, channels, channels).astype(jnp.float32)
    mixed_modes = jnp.einsum("kqi,kqio->kqo", coeffs, weights, precision=PRECISE)
    spatial, _ = to_planes(mixed_modes, inverse_x, inverse_t4, yz_table, steps_here)
    field_rows = field.reshape(-1, channels, plane_cells)
    linear = jnp.einsum(
        "io,riy->roy", point_weight, field_rows, preferred_element_type=jnp.float32
    ).reshape(spatial.shape)
    preact = spatial + linear + bias[None, None, :, None]
    normal_cdf = 0.5 * (1.0 + lax.erf(preact * SQRT_HALF))
    activated = (preact * normal_cdf).astype(jnp.bfloat16)
    slope = normal_cdf + preact * jnp.exp(-0.5 * preact * preact) * INV_ROOT_TWO_PI
    slopes = (cotangent.astype(jnp.float32) * slope).astype(jnp.bfloat16)
    slope_rows = slopes.reshape(-1, channels, plane_cells)
    weight_part = jnp.einsum("riy,roy->io", field_rows, slope_rows, preferred_element_type=jnp.float32)
    bias_part = jnp.sum(slopes.astype(jnp.float32), axis=(0, 1, 3))
    packed = jnp.concatenate([weight_part.reshape(-1), bias_part])
    packed = jnp.pad(packed, (0, Q - packed.shape[0]))
    slope_modes, packed_part = to_spectrum(slopes, yz_table, inverse_t4, inverse_x, extra=packed)
    spec_scale = math.sqrt(KX * Q / (grid_x * GY * GZ * GT))
    spectral_grad = (spec_scale * jnp.einsum("kqi,kqo->kqio", coeffs, slope_modes)).reshape(
        KX, -1, channels * channels
    )
    coeff_grad = jnp.einsum("kqio,kqo->kqi", weights, slope_modes, precision=PRECISE)
    grad_spatial, packed_sum = to_planes(
        coeff_grad, forward_x, forward_t, yz_table, steps_here, extra=packed_part, one_pass=True
    )
    cell_scale = 1.0 / math.sqrt(grid_x * GY * GZ * GT)
    weight_grad = cell_scale * packed_sum[: channels * channels].reshape(channels, channels)
    bias_grad = cell_scale * packed_sum[channels * channels : channels * channels + channels]
    point_part = jnp.einsum(
        "io,roy->riy", point_weight, slope_rows, preferred_element_type=jnp.float32
    ).reshape(grad_spatial.shape)
    field_grad = (grad_spatial + point_part).astype(jnp.bfloat16)
    return (activated, field_grad, spectral_grad, weight_grad, bias_grad)


def solution(mesh):
    return jax.shard_map(
        shards,
        mesh=mesh,
        in_specs=(
            P("ch", "sp", None, None),
            P(None, ("sp", "ch"), None),
            P(),
            P(),
            P("ch", "sp", None, None),
        ),
        out_specs=(
            P("ch", "sp", None, None),
            P("ch", "sp", None, None),
            P(None, ("sp", "ch"), None),
            P(),
            P(),
        ),
        check_vma=False,
    )
```

```python
import math

import jax
import jax.numpy as jnp
from jax import lax
from jax.sharding import PartitionSpec as P

KX = 16
KY = 16
KZ = 16
KT = 8
GY = 64
GZ = 64
GT = 32
KYZ = 256
Q = 2048
LANES = 128
SUB = 8


PRECISE = lax.Precision.HIGHEST
SQRT_HALF = 0.7071067811865476
INV_ROOT_TWO_PI = 0.3989422804014327


def wave_table(length, kept_rows, positions):
    row_ids = jnp.arange(kept_rows, dtype=jnp.int32)
    half_kept = kept_rows // 2
    frequency = jnp.where(row_ids <= half_kept, row_ids, row_ids - half_kept)
    phase_ids = frequency[:, None] * positions[None, :] % length
    angles = 2.0 * math.pi / length * phase_ids.astype(jnp.float32)
    waves = jnp.where((row_ids <= half_kept)[:, None], jnp.cos(angles), jnp.sin(angles))
    return math.sqrt(2.0 / length) * waves


def exact_spread(rows, selector):
    pieces = []
    rest = rows
    for _ in range(3):
        piece = lax.reduce_precision(rest, exponent_bits=8, mantissa_bits=7)
        rest = rest - piece
        pieces.append(piece.astype(jnp.bfloat16))
    stacked = jnp.concatenate([selector] * 3, axis=0)
    return jnp.dot(jnp.concatenate(pieces, axis=1), stacked, preferred_element_type=jnp.float32)


def plane_table():
    wave_y = wave_table(GY, KY, jnp.arange(GY, dtype=jnp.int32))
    wave_z = wave_table(GZ, KZ, jnp.arange(GZ, dtype=jnp.int32))
    y_rows = jnp.repeat(wave_y, KZ, axis=0)
    z_rows = jnp.tile(wave_z, (KY, 1))
    cells = jnp.arange(GY * GZ, dtype=jnp.int32)
    y_rows, z_rows, cells = lax.optimization_barrier((y_rows, z_rows, cells))
    pick_y = (cells[None, :] // GZ == jnp.arange(GY, dtype=jnp.int32)[:, None]).astype(jnp.bfloat16)
    pick_z = (cells[None, :] % GZ == jnp.arange(GZ, dtype=jnp.int32)[:, None]).astype(jnp.bfloat16)
    product = exact_spread(y_rows, pick_y) * exact_spread(z_rows, pick_z)
    return product.astype(jnp.bfloat16)


def split_dot(values, table):
    high = lax.reduce_precision(values, exponent_bits=8, mantissa_bits=7)
    low = (values - high).astype(jnp.bfloat16)
    return jnp.dot(high.astype(jnp.bfloat16), table, preferred_element_type=jnp.float32) + jnp.dot(
        low, table, preferred_element_type=jnp.float32
    )


def to_spectrum(values, yz_table, time_table, x_table, extra=None):
    steps_here, planes, channels, plane_cells = values.shape
    sp_count, ch_count = lax.axis_size("sp"), lax.axis_size("ch")
    own = Q // (sp_count * ch_count)
    rows_per = own * channels // LANES
    flat = jnp.einsum(
        "qc,rc->qr", yz_table, values.reshape(-1, plane_cells), preferred_element_type=jnp.float32
    ).reshape(KYZ, steps_here, channels)
    partial = jnp.einsum("kt,ptc->kpc", time_table, flat, precision=PRECISE)
    send = partial.reshape(sp_count * ch_count, rows_per, LANES)
    if extra is not None:
        rider = jnp.zeros((sp_count * ch_count, 1, LANES), jnp.float32)
        rider = rider.at[:, 0, :own].set(extra.reshape(-1, own))
        send = jnp.concatenate([send, rider], axis=1)
    arrived = lax.all_to_all(send, ("sp", "ch"), 0, 0, tiled=True)
    by_plane = arrived[:, :rows_per].reshape(sp_count, ch_count, rows_per, LANES)
    owned = jnp.einsum("kx,xmrl->krl", x_table, by_plane, precision=PRECISE)
    owned = owned.reshape(KX, own, channels)
    if extra is None:
        return owned
    return owned, jnp.sum(arrived[:, rows_per, :own], axis=0)


def to_planes(block, x_table, time_table, yz_table, steps_here, extra=None, one_pass=False):
    channels = block.shape[2]
    sp_count, ch_count = lax.axis_size("sp"), lax.axis_size("ch")
    own = block.shape[1]
    rows_per = own * channels // LANES
    rows = block.reshape(KX, rows_per, LANES)
    spread = jnp.einsum("kx,krl->xrl", x_table, rows, precision=PRECISE)
    if extra is not None:
        rider = jnp.zeros((sp_count, 1, LANES), jnp.float32).at[:, 0, :own].set(
            jnp.broadcast_to(extra[None], (sp_count, own))
        )
        spread = jnp.concatenate([spread, rider], axis=1)
    copies = jnp.broadcast_to(spread[:, None], (sp_count, ch_count) + spread.shape[1:])
    returned = lax.all_to_all(
        copies.reshape((-1,) + spread.shape[1:]), ("sp", "ch"), 0, 0, tiled=True
    )
    total = returned[:, rows_per, :own].reshape(-1) if extra is not None else None
    modes = returned[:, :rows_per].reshape(KT, KYZ, channels)
    time_spread = jnp.einsum("kt,kpo->top", time_table, modes, precision=PRECISE)
    time_spread = time_spread.reshape(-1, KYZ)
    if one_pass:
        result = jnp.dot(time_spread.astype(jnp.bfloat16), yz_table, preferred_element_type=jnp.float32)
    else:
        result = split_dot(time_spread, yz_table)
    return result.reshape(steps_here, 1, channels, -1), total


def shards(field, spectral_weight, point_weight, bias, cotangent):
    steps_here, planes, channels, plane_cells = field.shape
    sp_count = lax.axis_size("sp")
    grid_x = planes * sp_count
    forward_x = wave_table(grid_x, KX, jnp.arange(grid_x, dtype=jnp.int32))
    inverse_x = forward_x * math.sqrt(grid_x / KX)
    time_ids = lax.axis_index("ch") * steps_here + jnp.arange(steps_here, dtype=jnp.int32)
    forward_t = wave_table(GT, KT, time_ids)
    inverse_t = forward_t * math.sqrt(GT / KT)
    inverse_t4 = inverse_t * float(math.sqrt(GY / KY) * math.sqrt(GZ / KZ))
    yz_table = plane_table()
    coeffs = to_spectrum(field, yz_table, forward_t, forward_x)
    weights = spectral_weight.reshape(KX, -1, channels, channels).astype(jnp.float32)
    mixed_modes = jnp.einsum("kqi,kqio->kqo", coeffs, weights, precision=PRECISE)
    spatial, _ = to_planes(mixed_modes, inverse_x, inverse_t4, yz_table, steps_here)
    field_rows = field.reshape(-1, channels, plane_cells)
    linear = lax.optimization_barrier(
        jnp.einsum("io,riy->roy", point_weight, field_rows, preferred_element_type=jnp.float32)
    ).reshape(spatial.shape)
    preact = spatial + linear + bias[None, None, :, None]
    normal_cdf = 0.5 * (1.0 + lax.erf(preact * SQRT_HALF))
    activated = (preact * normal_cdf).astype(jnp.bfloat16)
    slope = normal_cdf + preact * jnp.exp(-0.5 * preact * preact) * INV_ROOT_TWO_PI
    slopes = (cotangent.astype(jnp.float32) * slope).astype(jnp.bfloat16)
    slope_rows = slopes.reshape(-1, channels, plane_cells)
    weight_part = jnp.einsum("riy,roy->io", field_rows, slope_rows, preferred_element_type=jnp.float32)
    bias_part = jnp.sum(slopes.astype(jnp.float32), axis=(0, 1, 3))
    packed = jnp.concatenate([weight_part.reshape(-1), bias_part])
    packed = jnp.pad(packed, (0, Q - packed.shape[0]))
    slope_modes, packed_part = to_spectrum(slopes, yz_table, inverse_t4, inverse_x, extra=packed)
    spec_scale = math.sqrt(KX * Q / (grid_x * GY * GZ * GT))
    spectral_grad = (spec_scale * jnp.einsum("kqi,kqo->kqio", coeffs, slope_modes)).reshape(
        KX, -1, channels * channels
    )
    coeff_grad = jnp.einsum("kqio,kqo->kqi", weights, slope_modes, precision=PRECISE)
    grad_spatial, packed_sum = to_planes(
        coeff_grad, forward_x, forward_t, yz_table, steps_here, extra=packed_part, one_pass=True
    )
    cell_scale = 1.0 / math.sqrt(grid_x * GY * GZ * GT)
    weight_grad = cell_scale * packed_sum[: channels * channels].reshape(channels, channels)
    bias_grad = cell_scale * packed_sum[channels * channels : channels * channels + channels]
    point_part = jnp.einsum(
        "io,roy->riy", point_weight, slope_rows, preferred_element_type=jnp.float32
    ).reshape(grad_spatial.shape)
    field_grad = (grad_spatial + point_part).astype(jnp.bfloat16)
    return (activated, field_grad, spectral_grad, weight_grad, bias_grad)


def solution(mesh):
    return jax.shard_map(
        shards,
        mesh=mesh,
        in_specs=(
            P("ch", "sp", None, None),
            P(None, ("sp", "ch"), None),
            P(),
            P(),
            P("ch", "sp", None, None),
        ),
        out_specs=(
            P("ch", "sp", None, None),
            P("ch", "sp", None, None),
            P(None, ("sp", "ch"), None),
            P(),
            P(),
        ),
        check_vma=False,
    )
```

```python
import math

import jax
import jax.numpy as jnp
from jax import lax
from jax.sharding import PartitionSpec as P

KX = 16
KY = 16
KZ = 16
KT = 8
GY = 64
GZ = 64
GT = 32
KYZ = 256
Q = 2048
LANES = 128
SUB = 8


PRECISE = lax.Precision.HIGHEST
SQRT_HALF = 0.7071067811865476
INV_ROOT_TWO_PI = 0.3989422804014327


def wave_table(length, kept_rows, positions):
    row_ids = jnp.arange(kept_rows, dtype=jnp.int32)
    half_kept = kept_rows // 2
    frequency = jnp.where(row_ids <= half_kept, row_ids, row_ids - half_kept)
    phase_ids = frequency[:, None] * positions[None, :] % length
    angles = 2.0 * math.pi / length * phase_ids.astype(jnp.float32)
    waves = jnp.where((row_ids <= half_kept)[:, None], jnp.cos(angles), jnp.sin(angles))
    return math.sqrt(2.0 / length) * waves


def exact_spread(rows, selector):
    pieces = []
    rest = rows
    for _ in range(3):
        piece = lax.reduce_precision(rest, exponent_bits=8, mantissa_bits=7)
        rest = rest - piece
        pieces.append(piece.astype(jnp.bfloat16))
    stacked = jnp.concatenate([selector] * 3, axis=0)
    return jnp.dot(jnp.concatenate(pieces, axis=1), stacked, preferred_element_type=jnp.float32)


def plane_table():
    wave_y = wave_table(GY, KY, jnp.arange(GY, dtype=jnp.int32))
    wave_z = wave_table(GZ, KZ, jnp.arange(GZ, dtype=jnp.int32))
    y_rows = jnp.repeat(wave_y, KZ, axis=0)
    z_rows = jnp.tile(wave_z, (KY, 1))
    cells = jnp.arange(GY * GZ, dtype=jnp.int32)
    y_rows, z_rows, cells = lax.optimization_barrier((y_rows, z_rows, cells))
    pick_y = (cells[None, :] // GZ == jnp.arange(GY, dtype=jnp.int32)[:, None]).astype(jnp.bfloat16)
    pick_z = (cells[None, :] % GZ == jnp.arange(GZ, dtype=jnp.int32)[:, None]).astype(jnp.bfloat16)
    product = exact_spread(y_rows, pick_y) * exact_spread(z_rows, pick_z)
    return product.astype(jnp.bfloat16)


def split_dot(values, table):
    high = lax.reduce_precision(values, exponent_bits=8, mantissa_bits=7)
    low = (values - high).astype(jnp.bfloat16)
    return jnp.dot(high.astype(jnp.bfloat16), table, preferred_element_type=jnp.float32) + jnp.dot(
        low, table, preferred_element_type=jnp.float32
    )


def to_spectrum(values, yz_table, time_table, x_table, extra=None):
    steps_here, planes, channels, plane_cells = values.shape
    sp_count, ch_count = lax.axis_size("sp"), lax.axis_size("ch")
    own = Q // (sp_count * ch_count)
    rows_per = own * channels // LANES
    flat = jnp.einsum(
        "qc,rc->qr", yz_table, values.reshape(-1, plane_cells), preferred_element_type=jnp.float32
    ).reshape(KYZ, steps_here, channels)
    partial = jnp.einsum("kt,ptc->kpc", time_table, flat, precision=PRECISE)
    send = partial.reshape(sp_count * ch_count, rows_per, LANES)
    if extra is not None:
        rider = jnp.zeros((sp_count * ch_count, 1, LANES), jnp.float32)
        rider = rider.at[:, 0, :own].set(extra.reshape(-1, own))
        send = jnp.concatenate([send, rider], axis=1)
    arrived = lax.all_to_all(send, ("sp", "ch"), 0, 0, tiled=True)
    by_plane = arrived[:, :rows_per].reshape(sp_count, ch_count, rows_per, LANES)
    owned = jnp.einsum("kx,xmrl->krl", x_table, by_plane, precision=PRECISE)
    owned = owned.reshape(KX, own, channels)
    if extra is None:
        return owned
    return owned, jnp.sum(arrived[:, rows_per, :own], axis=0)


def to_planes(block, x_table, time_table, yz_table, steps_here, extra=None, one_pass=False):
    channels = block.shape[2]
    sp_count, ch_count = lax.axis_size("sp"), lax.axis_size("ch")
    own = block.shape[1]
    rows_per = own * channels // LANES
    rows = block.reshape(KX, rows_per, LANES)
    spread = jnp.einsum("kx,krl->xrl", x_table, rows, precision=PRECISE)
    if extra is not None:
        rider = jnp.zeros((sp_count, 1, LANES), jnp.float32).at[:, 0, :own].set(
            jnp.broadcast_to(extra[None], (sp_count, own))
        )
        spread = jnp.concatenate([spread, rider], axis=1)
    copies = jnp.broadcast_to(spread[:, None], (sp_count, ch_count) + spread.shape[1:])
    returned = lax.all_to_all(
        copies.reshape((-1,) + spread.shape[1:]), ("sp", "ch"), 0, 0, tiled=True
    )
    total = returned[:, rows_per, :own].reshape(-1) if extra is not None else None
    modes = returned[:, :rows_per].reshape(KT, KYZ, channels)
    time_spread = jnp.einsum("kt,kpo->top", time_table, modes, precision=PRECISE)
    time_spread = time_spread.reshape(-1, KYZ)
    if one_pass:
        result = jnp.dot(time_spread.astype(jnp.bfloat16), yz_table, preferred_element_type=jnp.float32)
    else:
        result = split_dot(time_spread, yz_table)
    return result.reshape(steps_here, 1, channels, -1), total


def shards(field, spectral_weight, point_weight, bias, cotangent):
    steps_here, planes, channels, plane_cells = field.shape
    sp_count = lax.axis_size("sp")
    grid_x = planes * sp_count
    forward_x = wave_table(grid_x, KX, jnp.arange(grid_x, dtype=jnp.int32))
    inverse_x = forward_x * math.sqrt(grid_x / KX)
    time_ids = lax.axis_index("ch") * steps_here + jnp.arange(steps_here, dtype=jnp.int32)
    forward_t = wave_table(GT, KT, time_ids)
    inverse_t = forward_t * math.sqrt(GT / KT)
    inverse_t4 = inverse_t * float(math.sqrt(GY / KY) * math.sqrt(GZ / KZ))
    yz_table = plane_table()
    coeffs = to_spectrum(field, yz_table, forward_t, forward_x)
    weights = spectral_weight.reshape(KX, -1, channels, channels).astype(jnp.float32)
    mixed_modes = jnp.einsum("kqi,kqio->kqo", coeffs, weights, precision=PRECISE)
    spatial, _ = to_planes(mixed_modes, inverse_x, inverse_t4, yz_table, steps_here)
    field_rows = field.reshape(-1, channels, plane_cells)
    linear = jnp.einsum(
        "io,riy->roy", point_weight, field_rows, preferred_element_type=jnp.float32
    ).reshape(spatial.shape)
    preact = spatial + linear + bias[None, None, :, None]
    normal_cdf = 0.5 * (1.0 + lax.erf(preact * SQRT_HALF))
    activated = (preact * normal_cdf).astype(jnp.bfloat16)
    slope = normal_cdf + preact * jnp.exp(-0.5 * preact * preact) * INV_ROOT_TWO_PI
    slopes = (cotangent.astype(jnp.float32) * slope).astype(jnp.bfloat16)
    slope_rows = slopes.reshape(-1, channels, plane_cells)
    weight_part = jnp.einsum("riy,roy->io", field_rows, slope_rows, preferred_element_type=jnp.float32)
    bias_part = jnp.sum(slopes.astype(jnp.float32), axis=(0, 1, 3))
    packed = jnp.concatenate([weight_part.reshape(-1), bias_part])
    packed = jnp.pad(packed, (0, Q - packed.shape[0]))
    slope_modes, packed_part = to_spectrum(slopes, yz_table, inverse_t4, inverse_x, extra=packed)
    spec_scale = math.sqrt(KX * Q / (grid_x * GY * GZ * GT))
    spectral_grad = (spec_scale * jnp.einsum("kqi,kqo->kqio", coeffs, slope_modes)).reshape(
        KX, -1, channels * channels
    )
    coeff_grad = jnp.sum(weights * slope_modes[:, :, None, :], axis=3)
    grad_spatial, packed_sum = to_planes(
        coeff_grad, forward_x, forward_t, yz_table, steps_here, extra=packed_part, one_pass=True
    )
    cell_scale = 1.0 / math.sqrt(grid_x * GY * GZ * GT)
    weight_grad = cell_scale * packed_sum[: channels * channels].reshape(channels, channels)
    bias_grad = cell_scale * packed_sum[channels * channels : channels * channels + channels]
    point_part = jnp.einsum(
        "io,roy->riy", point_weight, slope_rows, preferred_element_type=jnp.float32
    ).reshape(grad_spatial.shape)
    field_grad = (grad_spatial + point_part).astype(jnp.bfloat16)
    return (activated, field_grad, spectral_grad, weight_grad, bias_grad)


def solution(mesh):
    return jax.shard_map(
        shards,
        mesh=mesh,
        in_specs=(
            P("ch", "sp", None, None),
            P(None, ("sp", "ch"), None),
            P(),
            P(),
            P("ch", "sp", None, None),
        ),
        out_specs=(
            P("ch", "sp", None, None),
            P("ch", "sp", None, None),
            P(None, ("sp", "ch"), None),
            P(),
            P(),
        ),
        check_vma=False,
    )
```

```python
import math

import jax
import jax.numpy as jnp
from jax import lax
from jax.sharding import PartitionSpec as P

KX = 16
KY = 16
KZ = 16
KT = 8
GY = 64
GZ = 64
GT = 32
KYZ = 256
Q = 2048
LANES = 128
SUB = 8


PRECISE = lax.Precision.HIGHEST
SQRT_HALF = 0.7071067811865476
INV_ROOT_TWO_PI = 0.3989422804014327


def wave_table(length, kept_rows, positions):
    row_ids = jnp.arange(kept_rows, dtype=jnp.int32)
    half_kept = kept_rows // 2
    frequency = jnp.where(row_ids <= half_kept, row_ids, row_ids - half_kept)
    phase_ids = frequency[:, None] * positions[None, :] % length
    angles = 2.0 * math.pi / length * phase_ids.astype(jnp.float32)
    waves = jnp.where((row_ids <= half_kept)[:, None], jnp.cos(angles), jnp.sin(angles))
    return math.sqrt(2.0 / length) * waves


def exact_spread(rows, selector):
    pieces = []
    rest = rows
    for _ in range(3):
        piece = lax.reduce_precision(rest, exponent_bits=8, mantissa_bits=7)
        rest = rest - piece
        pieces.append(piece.astype(jnp.bfloat16))
    stacked = jnp.concatenate([selector] * 3, axis=0)
    return jnp.dot(jnp.concatenate(pieces, axis=1), stacked, preferred_element_type=jnp.float32)


def plane_table():
    wave_y = wave_table(GY, KY, jnp.arange(GY, dtype=jnp.int32))
    wave_z = wave_table(GZ, KZ, jnp.arange(GZ, dtype=jnp.int32))
    y_rows = jnp.repeat(wave_y, KZ, axis=0)
    z_rows = jnp.tile(wave_z, (KY, 1))
    cells = jnp.arange(GY * GZ, dtype=jnp.int32)
    y_rows, z_rows, cells = lax.optimization_barrier((y_rows, z_rows, cells))
    pick_y = (cells[None, :] // GZ == jnp.arange(GY, dtype=jnp.int32)[:, None]).astype(jnp.bfloat16)
    pick_z = (cells[None, :] % GZ == jnp.arange(GZ, dtype=jnp.int32)[:, None]).astype(jnp.bfloat16)
    product = exact_spread(y_rows, pick_y) * exact_spread(z_rows, pick_z)
    return product.astype(jnp.bfloat16)


def split_dot(values, table):
    high = lax.reduce_precision(values, exponent_bits=8, mantissa_bits=7)
    low = (values - high).astype(jnp.bfloat16)
    pieces = jnp.concatenate([high.astype(jnp.bfloat16), low], axis=1)
    stacked = jnp.concatenate([table, table], axis=0)
    return jnp.dot(pieces, stacked, preferred_element_type=jnp.float32)


def to_spectrum(values, yz_table, time_table, x_table, extra=None):
    steps_here, planes, channels, plane_cells = values.shape
    sp_count, ch_count = lax.axis_size("sp"), lax.axis_size("ch")
    own = Q // (sp_count * ch_count)
    rows_per = own * channels // LANES
    flat = jnp.einsum(
        "qc,rc->qr", yz_table, values.reshape(-1, plane_cells), preferred_element_type=jnp.float32
    ).reshape(KYZ, steps_here, channels)
    partial = jnp.einsum("kt,ptc->kpc", time_table, flat, precision=PRECISE)
    send = partial.reshape(sp_count * ch_count, rows_per, LANES)
    if extra is not None:
        rider = jnp.zeros((sp_count * ch_count, 1, LANES), jnp.float32)
        rider = rider.at[:, 0, :own].set(extra.reshape(-1, own))
        send = jnp.concatenate([send, rider], axis=1)
    arrived = lax.all_to_all(send, ("sp", "ch"), 0, 0, tiled=True)
    by_plane = arrived[:, :rows_per].reshape(sp_count, ch_count, rows_per, LANES)
    owned = jnp.einsum("kx,xmrl->krl", x_table, by_plane, precision=PRECISE)
    owned = owned.reshape(KX, own, channels)
    if extra is None:
        return owned
    return owned, jnp.sum(arrived[:, rows_per, :own], axis=0)


def to_planes(block, x_table, time_table, yz_table, steps_here, extra=None, one_pass=False):
    channels = block.shape[2]
    sp_count, ch_count = lax.axis_size("sp"), lax.axis_size("ch")
    own = block.shape[1]
    rows_per = own * channels // LANES
    rows = block.reshape(KX, rows_per, LANES)
    spread = jnp.einsum("kx,krl->xrl", x_table, rows, precision=PRECISE)
    if extra is not None:
        rider = jnp.zeros((sp_count, 1, LANES), jnp.float32).at[:, 0, :own].set(
            jnp.broadcast_to(extra[None], (sp_count, own))
        )
        spread = jnp.concatenate([spread, rider], axis=1)
    copies = jnp.broadcast_to(spread[:, None], (sp_count, ch_count) + spread.shape[1:])
    returned = lax.all_to_all(
        copies.reshape((-1,) + spread.shape[1:]), ("sp", "ch"), 0, 0, tiled=True
    )
    total = returned[:, rows_per, :own].reshape(-1) if extra is not None else None
    modes = returned[:, :rows_per].reshape(KT, KYZ, channels)
    time_spread = jnp.einsum("kt,kpo->top", time_table, modes, precision=PRECISE)
    time_spread = time_spread.reshape(-1, KYZ)
    if one_pass:
        result = jnp.dot(time_spread.astype(jnp.bfloat16), yz_table, preferred_element_type=jnp.float32)
    else:
        result = split_dot(time_spread, yz_table)
    return result.reshape(steps_here, 1, channels, -1), total


def shards(field, spectral_weight, point_weight, bias, cotangent):
    steps_here, planes, channels, plane_cells = field.shape
    sp_count = lax.axis_size("sp")
    grid_x = planes * sp_count
    forward_x = wave_table(grid_x, KX, jnp.arange(grid_x, dtype=jnp.int32))
    inverse_x = forward_x * math.sqrt(grid_x / KX)
    time_ids = lax.axis_index("ch") * steps_here + jnp.arange(steps_here, dtype=jnp.int32)
    forward_t = wave_table(GT, KT, time_ids)
    inverse_t = forward_t * math.sqrt(GT / KT)
    inverse_t4 = inverse_t * float(math.sqrt(GY / KY) * math.sqrt(GZ / KZ))
    yz_table = plane_table()
    coeffs = to_spectrum(field, yz_table, forward_t, forward_x)
    weights = spectral_weight.reshape(KX, -1, channels, channels).astype(jnp.float32)
    mixed_modes = jnp.einsum("kqi,kqio->kqo", coeffs, weights, precision=PRECISE)
    spatial, _ = to_planes(mixed_modes, inverse_x, inverse_t4, yz_table, steps_here)
    field_rows = field.reshape(-1, channels, plane_cells)
    linear = jnp.einsum(
        "io,riy->roy", point_weight, field_rows, preferred_element_type=jnp.float32
    ).reshape(spatial.shape)
    preact = spatial + linear + bias[None, None, :, None]
    normal_cdf = 0.5 * (1.0 + lax.erf(preact * SQRT_HALF))
    activated = (preact * normal_cdf).astype(jnp.bfloat16)
    slope = normal_cdf + preact * jnp.exp(-0.5 * preact * preact) * INV_ROOT_TWO_PI
    slopes = (cotangent.astype(jnp.float32) * slope).astype(jnp.bfloat16)
    slope_rows = slopes.reshape(-1, channels, plane_cells)
    weight_part = jnp.einsum("riy,roy->io", field_rows, slope_rows, preferred_element_type=jnp.float32)
    bias_part = jnp.sum(slopes.astype(jnp.float32), axis=(0, 1, 3))
    packed = jnp.concatenate([weight_part.reshape(-1), bias_part])
    packed = jnp.pad(packed, (0, Q - packed.shape[0]))
    slope_modes, packed_part = to_spectrum(slopes, yz_table, inverse_t4, inverse_x, extra=packed)
    spec_scale = math.sqrt(KX * Q / (grid_x * GY * GZ * GT))
    spectral_grad = (spec_scale * jnp.einsum("kqi,kqo->kqio", coeffs, slope_modes)).reshape(
        KX, -1, channels * channels
    )
    coeff_grad = jnp.einsum("kqio,kqo->kqi", weights, slope_modes, precision=PRECISE)
    grad_spatial, packed_sum = to_planes(
        coeff_grad, forward_x, forward_t, yz_table, steps_here, extra=packed_part, one_pass=True
    )
    cell_scale = 1.0 / math.sqrt(grid_x * GY * GZ * GT)
    weight_grad = cell_scale * packed_sum[: channels * channels].reshape(channels, channels)
    bias_grad = cell_scale * packed_sum[channels * channels : channels * channels + channels]
    point_part = jnp.einsum(
        "io,roy->riy", point_weight, slope_rows, preferred_element_type=jnp.float32
    ).reshape(grad_spatial.shape)
    field_grad = (grad_spatial + point_part).astype(jnp.bfloat16)
    return (activated, field_grad, spectral_grad, weight_grad, bias_grad)


def solution(mesh):
    return jax.shard_map(
        shards,
        mesh=mesh,
        in_specs=(
            P("ch", "sp", None, None),
            P(None, ("sp", "ch"), None),
            P(),
            P(),
            P("ch", "sp", None, None),
        ),
        out_specs=(
            P("ch", "sp", None, None),
            P("ch", "sp", None, None),
            P(None, ("sp", "ch"), None),
            P(),
            P(),
        ),
        check_vma=False,
    )
```
